512 devices in a mesh: pulse: 128 (over x, z, core), chan: 4 (over y).
Axes of the slice: x: 4, y: 4, z: 16, core: 2. Of those that a mesh axis runs over, the one named last changes fastest.
Arguments:
- echoes: bfloat16 [16, 512, 2, 8192], P('chan', 'pulse'), may hold values from -6 to 6
- replica: bfloat16 [2, 4096], replicated, may hold values from -0.0625 to 0.0625
- recon_filters: bfloat16 [16, 16, 2, 64], replicated, may hold values from -0.125 to 0.125
- span_offset: int32 [1024], P('pulse'), may hold values from 0 to 4
- span_width: int32 [1024], P('pulse'), may hold values from 1 to 4
- aperture_edges: int32 [2, 1024], P(None, 'pulse'), may hold values from 0 to 64
Outputs:
- image: bfloat16 [16, 2, 1024, 512], P(None, None, 'pulse', 'chan')
The draws below stay inside these ranges and needn't reach their ends.
All inputs are finite; a program needn't handle non-finite values.
Results may differ from the reference program's by a relative error of at most 0.012.
Values may be sent and summed in bfloat16 or wider, within the bound.
No kernel may reach another device: no remote copies, remote signals or barrier semaphores. Data moves between devices by JAX's collectives and lax.ppermute only.
A program may use at most 64 MiB of HBM per device.

```python
import jax
import jax.numpy as jnp
from jax import lax

TAPS = 4096
AZ_TAPS = 64
MIG = 4
WMAX = 4
CHANNELS = 16
PULSES = 512
NR = 1024
SAMPLES = 8192
EDGE = 64


def plant(values, stream_key, low, largest):
    longest = values.shape.index(max(values.shape))
    spots = []
    for shift in (0, 1):
        where = [jax.random.randint(jax.random.fold_in(stream_key, axis), (), 0, length) for axis, length in enumerate(values.shape)]
        where[longest] = (where[longest] + shift) % values.shape[longest]
        spots.append(tuple(where))
    return values.at[spots[0]].set(low).at[spots[1]].set(largest)


def shard_levels(key, shape, pieces, low, high):
    level = 1.0
    for position, blocks in pieces:
        heights = jax.random.uniform(jax.random.fold_in(jax.random.fold_in(key, 6), position), (blocks,), jnp.float32, low / len(pieces), high / len(pieces))
        level = level * jnp.repeat(jnp.exp(heights), shape[position] // blocks).reshape((-1,) + (1,) * (len(shape) - 1 - position))
    return level


def noise(stream_key, dims, width, most, split=(), held_as=jnp.bfloat16):
    drawn = width * jax.random.normal(stream_key, dims, jnp.float32)
    if split:
        drawn = drawn * shard_levels(stream_key, dims, split, -0.22, 0.18)
    return jnp.clip(drawn, -most, most).astype(held_as)


def setup_inputs(seed: int = 0) -> dict:
    seeds = jax.random.split(jax.random.key(seed), 7)
    echoes = noise(seeds[0], (CHANNELS, PULSES, 2, SAMPLES), 1.0, 6.0, ((0, 4), (1, 128)))
    replica = noise(seeds[1], (2, TAPS), (2 * TAPS) ** -0.5, 0.0625)
    recon_filters = noise(seeds[2], (CHANNELS, CHANNELS, 2, AZ_TAPS), (2 * CHANNELS * AZ_TAPS) ** -0.5, 0.125)
    span_offset = plant(jax.random.randint(seeds[3], (NR,), 0, MIG + 1), jax.random.fold_in(seeds[3], 1), 0, MIG).astype(jnp.int32)
    span_width = plant(jax.random.randint(seeds[4], (NR,), 1, WMAX + 1), jax.random.fold_in(seeds[4], 1), 1, WMAX).astype(jnp.int32)
    aperture_edges = plant(jax.random.randint(seeds[5], (2, NR), 0, EDGE + 1), jax.random.fold_in(seeds[5], 1), 0, EDGE).astype(jnp.int32)
    return {"echoes": echoes, "replica": replica, "recon_filters": recon_filters, "span_offset": span_offset, "span_width": span_width, "aperture_edges": aperture_edges}


def to_complex(part_real, part_imag):
    return part_real.astype(jnp.float32) + 1j * part_imag.astype(jnp.float32)


def reference(echoes, replica, recon_filters, span_offset, span_width, aperture_edges):
    fft_len = SAMPLES + TAPS
    kernel_spec = jnp.fft.fft(to_complex(replica[0], replica[1])[::-1], fft_len)

    def range_line(channel):
        signal = to_complex(channel[:, 0], channel[:, 1])
        full = jnp.fft.ifft(jnp.fft.fft(signal, fft_len, axis=-1) * kernel_spec[None, :], axis=-1)
        picked = full[:, TAPS - 1:TAPS - 1 + 4 * NR:4]
        return jnp.stack([jnp.real(picked).astype(jnp.bfloat16), jnp.imag(picked).astype(jnp.bfloat16)], 0)

    compressed = lax.map(range_line, echoes)
    rim_len = MIG + WMAX - 1
    padded = jnp.pad(compressed.astype(jnp.float32), ((0, 0), (0, 0), (0, 0), (0, rim_len)))
    bin_ids = jnp.arange(NR, dtype=jnp.int32)
    span_first = (bin_ids + span_offset).astype(jnp.int32)
    scale = 1.0 / span_width.astype(jnp.float32)
    migrated = jnp.zeros((CHANNELS, 2, PULSES, NR), jnp.float32)
    for shift_step in range(WMAX):
        taken = jnp.take(padded, span_first + shift_step, axis=3)
        factor = jnp.where(shift_step < span_width, scale, 0.0)
        migrated = migrated + taken * factor
    pulse_ids = jnp.arange(PULSES, dtype=jnp.int32)[:, None]
    keep_mask = ((pulse_ids >= aperture_edges[0][None, :]) & (pulse_ids < PULSES - aperture_edges[1][None, :])).astype(jnp.float32)
    corrected = (migrated * keep_mask).astype(jnp.bfloat16)
    field = to_complex(corrected[:, 0], corrected[:, 1]).transpose(0, 2, 1)
    half_taps = AZ_TAPS // 2
    field = jnp.pad(field, ((0, 0), (0, 0), (half_taps, half_taps)))
    az_len = PULSES + 2 * AZ_TAPS
    field_spec = jnp.fft.fft(field, az_len, axis=-1)
    filter_spec = jnp.fft.fft(to_complex(recon_filters[:, :, 0], recon_filters[:, :, 1])[..., ::-1], az_len, axis=-1)
    image_spec = jnp.einsum('crl,scl->srl', field_spec, filter_spec, precision=lax.Precision.HIGHEST)
    image = jnp.fft.ifft(image_spec, axis=-1)[:, :, AZ_TAPS - 1:AZ_TAPS - 1 + PULSES]
    return jnp.stack([jnp.real(image), jnp.imag(image)], 1).astype(jnp.bfloat16)
```

```python
import functools

import jax
import jax.numpy as jnp
from jax import lax
from jax.experimental import pallas as pl
from jax.experimental.pallas import tpu as pltpu
from jax.sharding import PartitionSpec as P

F32 = jnp.float32
BF16 = jnp.bfloat16
LANES = 128
NT = (((1,), (1,)), ((), ()))


def lane_ids(rows):
    return lax.broadcasted_iota(jnp.int32, (rows, LANES), 1)


def swap_blocks(arrays, width):
    arrays = list(arrays)
    group = lane_ids(arrays[0].shape[0]) // width
    bit = 1
    while bit < len(arrays):
        low = (group & bit) == 0
        shift = bit * width
        for first in range(len(arrays)):
            if first & bit:
                continue
            second = first | bit
            a, b = arrays[first], arrays[second]
            arrays[first] = jnp.where(low, a, pltpu.roll(b, shift, 1))
            arrays[second] = jnp.where(low, pltpu.roll(a, LANES - shift, 1), b)
        bit *= 2
    return arrays


def compress_kernel(echo_ref, replica_ref, out_ref, taps, windows, parts, rows, chunks):
    lane = lane_ids(32)
    shift = 4 * lax.broadcasted_iota(jnp.int32, (32, LANES), 0)
    zero = jnp.zeros((32, LANES), F32)
    for part in range(2):
        previous = zero
        for m in range(33):
            if m < 32:
                row = replica_ref[part : part + 1, m * LANES : (m + 1) * LANES].astype(F32)
                rolled = pltpu.roll(
                    jnp.broadcast_to(row, (32, LANES)), 0, 1, stride=4, stride_axis=0
                )
            else:
                rolled = zero
            tile = jnp.where(lane >= shift, rolled, previous).astype(BF16)
            previous = rolled
            for a in range(4):
                taps[
                    part * 128 + 32 * a : part * 128 + 32 * a + 32,
                    (m + a) * LANES : (m + a + 1) * LANES,
                ] = tile
        for a in range(4):
            base = part * 128 + 32 * a
            if a:
                taps[base : base + 32, : a * LANES] = jnp.zeros((32, a * LANES), BF16)
            if a < 3:
                taps[base : base + 32, (33 + a) * LANES :] = jnp.zeros(
                    (32, (3 - a) * LANES), BF16
                )
    for part in range(2):
        for w in range(8):
            at = part * 128 + w * 16
            windows[at : at + 16, :] = echo_ref[part, :, 512 * w : 512 * w + 4608]
    product = lax.dot_general(taps[...], windows[...], NT, preferred_element_type=F32)
    parts[0:128, :] = product[:128, :128] - product[128:, 128:]
    parts[128:256, :] = product[:128, 128:] + product[128:, :128]
    pieces = [parts[pl.ds(128 * (g % 2) + g // 2, 32, stride=4), :] for g in range(8)]
    for w, piece in enumerate(swap_blocks(pieces, 16)):
        rows[32 * w : 32 * w + 32, :] = piece
    rows[256:264, :] = jnp.zeros((8, LANES), F32)
    for k in range(4):
        chunks[pl.ds(k, 128, stride=4), :] = rows[pl.ds(k, 128, stride=2), :]
    out_ref[...] = chunks[...].astype(BF16)


def compress(echo_rows, replica):
    return pl.pallas_call(
        compress_kernel,
        out_shape=jax.ShapeDtypeStruct((512, LANES), BF16),
        scratch_shapes=[
            pltpu.VMEM((256, 4608), BF16),
            pltpu.VMEM((256, 4608), BF16),
            pltpu.VMEM((256, LANES), F32),
            pltpu.VMEM((264, LANES), F32),
            pltpu.VMEM((512, LANES), F32),
        ],
        compiler_params=pltpu.CompilerParams(vmem_limit_bytes=24 << 20),
        cost_estimate=pl.CostEstimate(
            flops=2 * 256 * 256 * 4608, bytes_accessed=1 << 20, transcendentals=0
        ),
        name="compress",
    )(echo_rows, replica)


def migrate_kernel(turned_ref, info_ref, out_ref, quads, rows):
    quads[...] = turned_ref[...].astype(F32)
    quad = [quads[pl.ds(k, 128, stride=4), :] for k in range(4)]
    lane = lane_ids(128)
    group = lane // 32
    pulse = 4 * lax.broadcasted_iota(jnp.int32, (128, LANES), 0) + lane % 4
    shifted = [quad]
    for f in range(1, 4):
        rolled = [pltpu.roll(q, LANES - 32 * f, 1) for q in quad]
        shifted.append([jnp.where(group < 4 - f, rolled[k], rolled[k + 1]) for k in range(3)])
    rows[0:16, :] = jnp.zeros((16, LANES), F32)
    rows[272:288, :] = jnp.zeros((16, LANES), F32)
    for half in range(2):
        first = info_ref[half : half + 1, :]
        width = info_ref[2 + half : 3 + half, :]
        low = info_ref[4 + half : 5 + half, :]
        high = info_ref[6 + half : 7 + half, :]
        total = jnp.zeros((128, LANES), F32)
        for step in range(8):
            inside = (first <= step) & (step < first + width)
            total = total + jnp.where(inside, shifted[step % 4][half + step // 4], 0.0)
        total = total * (1.0 / width.astype(F32))
        keep = (pulse >= low) & (pulse < 512 - high)
        rows[pl.ds(16 + half, 128, stride=2), :] = jnp.where(keep, total, 0.0)
    for y in range(4):
        out_ref[96 * y : 96 * y + 96, :] = rows[64 * y : 64 * y + 96, :].astype(BF16)


def migrate(turned, info):
    return pl.pallas_call(
        migrate_kernel,
        out_shape=jax.ShapeDtypeStruct((384, LANES), BF16),
        scratch_shapes=[pltpu.VMEM((512, LANES), F32), pltpu.VMEM((288, LANES), F32)],
        cost_estimate=pl.CostEstimate(flops=1 << 20, bytes_accessed=1 << 18, transcendentals=0),
        name="migrate",
    )(turned, info)


def bands_kernel(filter_ref, out_ref, table):
    group = lane_ids(32) // 32
    zero = jnp.zeros((32, LANES), F32)

    def tap(t):
        return filter_ref[t].astype(F32) if 0 <= t < 64 else zero

    for m in range(72):
        block = tap(m)
        for jo in range(1, 4):
            block = jnp.where(group == jo, tap(m - jo), block)
        table[pl.ds(128 * (m // 4) + m % 4, 32, stride=4), :] = block
    out_ref[...] = table[...].astype(BF16)


def bands(filter_table):
    return pl.pallas_call(
        bands_kernel,
        out_shape=jax.ShapeDtypeStruct((2304, LANES), BF16),
        scratch_shapes=[pltpu.VMEM((2304, LANES), F32)],
        cost_estimate=pl.CostEstimate(flops=1 << 20, bytes_accessed=1 << 20, transcendentals=0),
        name="bands",
    )(filter_table)


def azimuth_kernel(turned_ref, bands_ref, out_ref, field, pair, result, planes, final):
    arrays = [turned_ref[96 * y : 96 * y + 96, :].astype(F32) for y in range(4)]
    for il, piece in enumerate(swap_blocks(arrays, 32)):
        field[pl.ds(il, 96, stride=4), :] = piece
    field[384:392, :] = jnp.zeros((8, LANES), F32)
    pair[:, :LANES] = field[0:384, :].astype(BF16)
    pair[:, LANES:] = field[8:392, :].astype(BF16)
    total = jnp.zeros((256, LANES), F32)
    for e in range(9):
        total = total + jnp.dot(
            pair[16 * e : 16 * e + 256, :],
            bands_ref[256 * e : 256 * e + 256, :],
            preferred_element_type=F32,
        )
    result[...] = total
    for half in range(2):
        arrays = [result[pl.ds(4 * half + i, 32, stride=8), :] for i in range(4)]
        for jo, piece in enumerate(swap_blocks(arrays, 32)):
            planes[pl.ds(128 * half + jo, 32, stride=4), :] = piece
        turned = planes[128 * half : 128 * half + 128, :].T
        for i in range(4):
            final[pl.ds(4 * half + i, 32, stride=8), :] = turned[32 * i : 32 * i + 32, :]
    out_ref[...] = final[...].astype(BF16)


def azimuth(turned, band_matrix):
    return pl.pallas_call(
        azimuth_kernel,
        out_shape=jax.ShapeDtypeStruct((256, LANES), BF16),
        scratch_shapes=[
            pltpu.VMEM((392, LANES), F32),
            pltpu.VMEM((384, 256), BF16),
            pltpu.VMEM((256, LANES), F32),
            pltpu.VMEM((256, LANES), F32),
            pltpu.VMEM((256, LANES), F32),
        ],
        cost_estimate=pl.CostEstimate(
            flops=2 * 256 * 128 * 2304, bytes_accessed=1 << 20, transcendentals=0
        ),
        name="azimuth",
    )(turned, band_matrix)


def filter_table(recon_filters):
    by_tap = recon_filters.reshape(16, 4, 4, 2, 64).transpose(4, 1, 2, 3, 0)
    real, imag = by_tap[:, :, :, 0], by_tap[:, :, :, 1]
    from_real = jnp.stack([real, imag], -1).reshape(64, 4, 1, 4, 32)
    from_imag = jnp.stack([-imag, real], -1).reshape(64, 4, 1, 4, 32)
    table = jnp.concatenate([from_real, from_imag], 2).reshape(64, 32, 32)
    return jnp.tile(table, (1, 1, 4))


def bin_info(span_offset, span_width, aperture_edges):
    info = jnp.stack([span_offset, span_width, aperture_edges[0], aperture_edges[1]], 0)
    return jnp.repeat(info.reshape(8, 4), 32, axis=1)


def body(echoes, replica, recon_filters, span_offset, span_width, aperture_edges):
    echo_rows = echoes.transpose(2, 0, 1, 3).reshape(2, 16, 8192)
    chunks = compress(echo_rows, replica)
    turned = lax.all_to_all(chunks.reshape(128, 4, LANES), "pulse", 0, 0, tiled=True)
    info = bin_info(span_offset, span_width, aperture_edges)
    band_matrix = bands(filter_table(recon_filters))
    corrected = migrate(turned.reshape(512, LANES), info)
    gathered = lax.all_to_all(corrected.reshape(4, 96, LANES), "chan", 0, 0, tiled=True)
    image = azimuth(gathered.reshape(384, LANES), band_matrix)
    return image.reshape(16, 2, 8, LANES)


def solution(mesh):
    return jax.shard_map(
        body,
        mesh=mesh,
        in_specs=(
            P("chan", "pulse", None, None),
            P(),
            P(),
            P("pulse"),
            P("pulse"),
            P(None, "pulse"),
        ),
        out_specs=P(None, None, "pulse", "chan"),
        check_vma=False,
    )
```

```python
import jax
import jax.numpy as jnp
from jax import lax
from jax.experimental import pallas as pl
from jax.experimental.pallas import tpu as pltpu
from jax.sharding import Mesh
from jax.sharding import PartitionSpec as P

F32 = jnp.float32
BF16 = jnp.bfloat16
LANES = 128
NT = (((1,), (1,)), ((), ()))


def lane_ids(rows):
    return lax.broadcasted_iota(jnp.int32, (rows, LANES), 1)


def swap_blocks(arrays, width):
    arrays = list(arrays)
    group = lane_ids(arrays[0].shape[0]) // width
    bit = 1
    while bit < len(arrays):
        low = (group & bit) == 0
        shift = bit * width
        for first in range(len(arrays)):
            if first & bit:
                continue
            second = first | bit
            a, b = arrays[first], arrays[second]
            arrays[first] = jnp.where(low, a, pltpu.roll(b, shift, 1))
            arrays[second] = jnp.where(low, pltpu.roll(a, LANES - shift, 1), b)
        bit *= 2
    return arrays


def compress_kernel(echo_ref, replica_ref, out_ref, taps, windows, parts, rows, chunks):
    lane = lane_ids(32)
    shift = 4 * lax.broadcasted_iota(jnp.int32, (32, LANES), 0)
    zero = jnp.zeros((32, LANES), F32)
    for part in range(2):
        previous = zero
        for m in range(33):
            if m < 32:
                row = replica_ref[part : part + 1, m * LANES : (m + 1) * LANES].astype(F32)
                rolled = pltpu.roll(
                    jnp.broadcast_to(row, (32, LANES)), 0, 1, stride=4, stride_axis=0
                )
            else:
                rolled = zero
            tile = jnp.where(lane >= shift, rolled, previous).astype(BF16)
            previous = rolled
            for a in range(4):
                taps[
                    part * 128 + 32 * a : part * 128 + 32 * a + 32,
                    (m + a) * LANES : (m + a + 1) * LANES,
                ] = tile
        for a in range(4):
            base = part * 128 + 32 * a
            if a:
                taps[base : base + 32, : a * LANES] = jnp.zeros((32, a * LANES), BF16)
            if a < 3:
                taps[base : base + 32, (33 + a) * LANES :] = jnp.zeros(
                    (32, (3 - a) * LANES), BF16
                )
    for part in range(2):
        for w in range(8):
            at = part * 128 + w * 16
            windows[at : at + 16, :] = echo_ref[part, :, 512 * w : 512 * w + 4608]
    product = lax.dot_general(taps[...], windows[...], NT, preferred_element_type=F32)
    parts[0:128, :] = product[:128, :128] - product[128:, 128:]
    parts[128:256, :] = product[:128, 128:] + product[128:, :128]
    pieces = [parts[pl.ds(128 * (g % 2) + g // 2, 32, stride=4), :] for g in range(8)]
    for w, piece in enumerate(swap_blocks(pieces, 16)):
        rows[32 * w : 32 * w + 32, :] = piece
    rows[256:264, :] = jnp.zeros((8, LANES), F32)
    for k in range(6):
        chunks[:, k, :] = rows[pl.ds(k, 64, stride=4), :]
    out_ref[...] = chunks[:, 0:6, :].astype(BF16)


def compress(echo_rows, replica):
    return pl.pallas_call(
        compress_kernel,
        out_shape=jax.ShapeDtypeStruct((64, 6, LANES), BF16),
        scratch_shapes=[
            pltpu.VMEM((256, 4608), BF16),
            pltpu.VMEM((256, 4608), BF16),
            pltpu.VMEM((256, LANES), F32),
            pltpu.VMEM((264, LANES), F32),
            pltpu.VMEM((64, 8, LANES), F32),
        ],
        compiler_params=pltpu.CompilerParams(vmem_limit_bytes=16 << 20),
        cost_estimate=pl.CostEstimate(
            flops=2 * 256 * 256 * 4608, bytes_accessed=1 << 20, transcendentals=0
        ),
        name="compress",
    )(echo_rows, replica)


def regroup_kernel(turned_ref, out_ref, quads, rows):
    quads[:, 0:6, :] = turned_ref[...].astype(F32)
    for core in range(2):
        rows[core, 0:16, :] = jnp.zeros((16, LANES), F32)
        rows[core, 272:288, :] = jnp.zeros((16, LANES), F32)
        for k in range(4):
            rows[core, pl.ds(16 + k, 64, stride=4), :] = quads[:, 2 * core + k, :]
    for y in range(4):
        for core in range(2):
            at = 96 * (2 * y + core)
            out_ref[at : at + 96, :] = rows[core, 64 * y : 64 * y + 96, :].astype(BF16)


def regroup(turned):
    return pl.pallas_call(
        regroup_kernel,
        out_shape=jax.ShapeDtypeStruct((768, LANES), BF16),
        scratch_shapes=[pltpu.VMEM((64, 8, LANES), F32), pltpu.VMEM((2, 288, LANES), F32)],
        compiler_params=pltpu.CompilerParams(vmem_limit_bytes=8 << 20),
        cost_estimate=pl.CostEstimate(flops=1 << 18, bytes_accessed=1 << 18, transcendentals=0),
        name="regroup",
    )(turned)


def bands_kernel(filter_ref, out_ref, table):
    group = lane_ids(32) // 32
    zero = jnp.zeros((32, LANES), F32)

    def tap(t):
        return filter_ref[t].astype(F32) if 0 <= t < 64 else zero

    for m in range(72):
        block = tap(m)
        for jo in range(1, 4):
            block = jnp.where(group == jo, tap(m - jo), block)
        table[pl.ds(128 * (m // 4) + m % 4, 32, stride=4), :] = block
    out_ref[...] = table[...].astype(BF16)


def bands(filter_table):
    return pl.pallas_call(
        bands_kernel,
        out_shape=jax.ShapeDtypeStruct((2304, LANES), BF16),
        scratch_shapes=[pltpu.VMEM((2304, LANES), F32)],
        compiler_params=pltpu.CompilerParams(vmem_limit_bytes=8 << 20),
        cost_estimate=pl.CostEstimate(flops=1 << 20, bytes_accessed=1 << 20, transcendentals=0),
        name="bands",
    )(filter_table)


def migrate(quad, info_ref, pulse):
    rows = quad[0].shape[0]
    group = lane_ids(rows) // 32
    shifted = [quad]
    for f in range(1, 4):
        rolled = [pltpu.roll(q, LANES - 32 * f, 1) for q in quad]
        shifted.append([jnp.where(group < 4 - f, rolled[k], rolled[k + 1]) for k in range(3)])
    halves = []
    for half in range(2):
        first = info_ref[half : half + 1, :]
        width = info_ref[2 + half : 3 + half, :]
        low = info_ref[4 + half : 5 + half, :]
        high = info_ref[6 + half : 7 + half, :]
        total = jnp.zeros((rows, LANES), F32)
        for step in range(8):
            inside = (first <= step) & (step < first + width)
            total = total + jnp.where(inside, shifted[step % 4][half + step // 4], 0.0)
        total = total * (1.0 / width.astype(F32))
        halves.append(jnp.where((pulse >= low) & (pulse < high), total, 0.0))
    return halves


def azimuth_kernel(
    turned_ref, info_ref, bands_ref, out_ref, quads, field, pair, result, planes, final
):
    quads[...] = turned_ref[...].astype(F32)
    slot = lax.broadcasted_iota(jnp.int32, (24, LANES), 0)
    for core in range(2):
        pulse = 8 * slot + 4 * core + lane_ids(24) % 4
        halves = []
        for y in range(4):
            at = 96 * (2 * y + core)
            quad = [quads[pl.ds(at + k, 24, stride=4), :] for k in range(4)]
            halves.append(migrate(quad, info_ref, pulse))
        for half in range(2):
            for il, piece in enumerate(swap_blocks([h[half] for h in halves], 32)):
                field[pl.ds(8 * core + 4 * half + il, 24, stride=16), :] = piece
    field[384:392, :] = jnp.zeros((8, LANES), F32)
    pair[:, :LANES] = field[0:384, :].astype(BF16)
    pair[:, LANES:] = field[8:392, :].astype(BF16)
    total = jnp.zeros((256, LANES), F32)
    for e in range(9):
        total = total + jnp.dot(
            pair[16 * e : 16 * e + 256, :],
            bands_ref[256 * e : 256 * e + 256, :],
            preferred_element_type=F32,
        )
    result[...] = total
    for half in range(2):
        arrays = [result[pl.ds(4 * half + i, 32, stride=8), :] for i in range(4)]
        for jo, piece in enumerate(swap_blocks(arrays, 32)):
            planes[pl.ds(128 * half + jo, 32, stride=4), :] = piece
        turned = planes[128 * half : 128 * half + 128, :].T
        for i in range(4):
            final[pl.ds(4 * half + i, 32, stride=8), :] = turned[32 * i : 32 * i + 32, :]
    out_ref[...] = final[...].astype(BF16)


def azimuth(turned, info, band_matrix):
    return pl.pallas_call(
        azimuth_kernel,
        out_shape=jax.ShapeDtypeStruct((256, LANES), BF16),
        scratch_shapes=[
            pltpu.VMEM((768, LANES), F32),
            pltpu.VMEM((392, LANES), F32),
            pltpu.VMEM((384, 256), BF16),
            pltpu.VMEM((256, LANES), F32),
            pltpu.VMEM((256, LANES), F32),
            pltpu.VMEM((256, LANES), F32),
        ],
        cost_estimate=pl.CostEstimate(
            flops=2 * 256 * 128 * 2304, bytes_accessed=1 << 20, transcendentals=0
        ),
        compiler_params=pltpu.CompilerParams(vmem_limit_bytes=8 << 20),
        name="azimuth",
    )(turned, info, band_matrix)


def filter_table(recon_filters):
    by_tap = recon_filters.reshape(16, 4, 4, 2, 64).transpose(4, 1, 2, 3, 0)
    real, imag = by_tap[:, :, :, 0], by_tap[:, :, :, 1]
    from_real = jnp.stack([real, imag], -1).reshape(64, 4, 1, 4, 32)
    from_imag = jnp.stack([-imag, real], -1).reshape(64, 4, 1, 4, 32)
    table = jnp.concatenate([from_real, from_imag], 2).reshape(64, 32, 32)
    return jnp.tile(table, (1, 1, 4))


def bin_info(span_offset, span_width, aperture_edges):
    origin = 128 * lax.axis_index("chan") - 32
    info = jnp.stack(
        [span_offset, span_width, aperture_edges[0] - origin, 512 - aperture_edges[1] - origin], 0
    )
    return jnp.repeat(info.reshape(8, 4), 32, axis=1)


def body(echoes, replica, recon_filters, span_offset, span_width, aperture_edges):
    echo_rows = echoes.transpose(2, 0, 1, 3).reshape(2, 16, 8192)
    chunks = compress(echo_rows, replica)
    turned = lax.all_to_all(chunks, "slot", 0, 0, tiled=True)
    info = bin_info(span_offset, span_width, aperture_edges)
    band_matrix = bands(filter_table(recon_filters))
    windows = regroup(turned)
    gathered = lax.all_to_all(
        windows.reshape(8, 96, LANES), ("chan", "core"), 0, 0, tiled=True
    )
    image = azimuth(gathered.reshape(768, LANES), info, band_matrix)
    return image.reshape(16, 2, 8, LANES)


def solution(mesh):
    split = Mesh(mesh.devices.reshape(64, 2, 4), ("slot", "core", "chan"))
    pulse = ("slot", "core")
    return jax.shard_map(
        body,
        mesh=split,
        in_specs=(
            P("chan", pulse, None, None),
            P(),
            P(),
            P(pulse),
            P(pulse),
            P(None, pulse),
        ),
        out_specs=P(None, None, pulse, "chan"),
        check_vma=False,
    )
```

```python
import jax
import jax.numpy as jnp
from jax import lax
from jax.experimental import pallas as pl
from jax.experimental.pallas import tpu as pltpu
from jax.sharding import Mesh
from jax.sharding import PartitionSpec as P

F32 = jnp.float32
BF16 = jnp.bfloat16
LANES = 128
NT = (((1,), (1,)), ((), ()))
FIRST = 41
LAST = ((2, 0), (2, 1), (3, 0), (3, 1), (0, 0), (0, 1), (1, 0), (1, 1))
SEGMENTS = ((0, FIRST, 64 - FIRST), (64 - FIRST, 0, FIRST))


def lane_ids(rows):
    return lax.broadcasted_iota(jnp.int32, (rows, LANES), 1)


def swap_blocks(arrays, width):
    arrays = list(arrays)
    group = lane_ids(arrays[0].shape[0]) // width
    bit = 1
    while bit < len(arrays):
        low = (group & bit) == 0
        shift = bit * width
        for first in range(len(arrays)):
            if first & bit:
                continue
            second = first | bit
            a, b = arrays[first], arrays[second]
            arrays[first] = jnp.where(low, a, pltpu.roll(b, shift, 1))
            arrays[second] = jnp.where(low, pltpu.roll(a, LANES - shift, 1), b)
        bit *= 2
    return arrays


def compress_kernel(
    echo_ref, replica_hbm, out_ref, replica_ref, echo_rows, sems, taps, windows, parts, rows, chunks
):
    taps_copy = pltpu.make_async_copy(replica_hbm, replica_ref, sems.at[16])
    taps_copy.start()
    copies = [
        pltpu.make_async_copy(
            echo_ref.at[row // 4, row % 4], echo_rows.at[pl.ds(2 * row, 2), :], sems.at[row]
        )
        for row in range(16)
    ]
    for copy in copies:
        copy.start()
    taps_copy.wait()
    lane = lane_ids(32)
    shift = 4 * lax.broadcasted_iota(jnp.int32, (32, LANES), 0)
    zero = jnp.zeros((32, LANES), F32)
    for part in range(2):
        previous = zero
        for m in range(33):
            if m < 32:
                row = replica_ref[part : part + 1, m * LANES : (m + 1) * LANES].astype(F32)
                rolled = pltpu.roll(
                    jnp.broadcast_to(row, (32, LANES)), 0, 1, stride=4, stride_axis=0
                )
            else:
                rolled = zero
            tile = jnp.where(lane >= shift, rolled, previous).astype(BF16)
            previous = rolled
            for a in range(4):
                taps[
                    part * 128 + 32 * a : part * 128 + 32 * a + 32,
                    (m + a) * LANES : (m + a + 1) * LANES,
                ] = tile
        for a in range(4):
            base = part * 128 + 32 * a
            if a:
                taps[base : base + 32, : a * LANES] = jnp.zeros((32, a * LANES), BF16)
            if a < 3:
                taps[base : base + 32, (33 + a) * LANES :] = jnp.zeros(
                    (32, (3 - a) * LANES), BF16
                )
    for copy in copies:
        copy.wait()
    for w in range(8):
        windows[32 * w : 32 * w + 32, :] = echo_rows[:, 512 * w : 512 * w + 4608]
    product = lax.dot_general(taps[...], windows[...], NT, preferred_element_type=F32)
    real_lane = lane_ids(128) % 2 == 0
    for half in range(2):
        by_real = product[:128, 128 * half : 128 * half + 128]
        by_imag = product[128:, 128 * half : 128 * half + 128]
        parts[128 * half : 128 * half + 128, :] = by_real + jnp.where(
            real_lane, -pltpu.roll(by_imag, LANES - 1, 1), pltpu.roll(by_imag, 1, 1)
        )
        pieces = [parts[pl.ds(128 * half + il, 32, stride=4), :] for il in range(4)]
        for w, piece in enumerate(swap_blocks(pieces, 32)):
            at = 128 * half + 32 * w
            rows[at : at + 32, :] = piece
    rows[256:264, :] = jnp.zeros((8, LANES), F32)
    for at, slot, count in SEGMENTS:
        for k in range(6):
            chunks[at : at + count, k, :] = rows[pl.ds(4 * slot + k, count, stride=4), :]
    out_ref[...] = chunks[:, 0:6, :].astype(BF16)


def compress(echoes, replica):
    return pl.pallas_call(
        compress_kernel,
        out_shape=jax.ShapeDtypeStruct((64, 6, LANES), BF16),
        in_specs=[
            pl.BlockSpec(memory_space=pl.ANY),
            pl.BlockSpec(memory_space=pl.ANY),
        ],
        scratch_shapes=[
            pltpu.VMEM((2, 4096), BF16),
            pltpu.VMEM((32, 8192), BF16),
            pltpu.SemaphoreType.DMA((17,)),
            pltpu.VMEM((256, 4608), BF16),
            pltpu.VMEM((256, 4608), BF16),
            pltpu.VMEM((256, LANES), F32),
            pltpu.VMEM((264, LANES), F32),
            pltpu.VMEM((64, 8, LANES), F32),
        ],
        compiler_params=pltpu.CompilerParams(vmem_limit_bytes=60 << 20),
        cost_estimate=pl.CostEstimate(
            flops=2 * 256 * 256 * 4608, bytes_accessed=1 << 20, transcendentals=0
        ),
        name="compress",
    )(echoes, replica)


def regroup_kernel(turned_ref, out_ref, quads, rows):
    quads[:, 0:6, :] = turned_ref[...].astype(F32)
    for core in range(2):
        rows[core, 0:16, :] = jnp.zeros((16, LANES), F32)
        rows[core, 272:288, :] = jnp.zeros((16, LANES), F32)
        for at, slot, count in SEGMENTS:
            for k in range(4):
                rows[core, pl.ds(16 + 4 * slot + k, count, stride=4), :] = quads[
                    at : at + count, 2 * core + k, :
                ]
    for at, (y, core) in enumerate(LAST):
        out_ref[96 * at : 96 * at + 96, :] = rows[core, 64 * y : 64 * y + 96, :].astype(BF16)


def regroup(turned):
    return pl.pallas_call(
        regroup_kernel,
        out_shape=jax.ShapeDtypeStruct((768, LANES), BF16),
        scratch_shapes=[pltpu.VMEM((64, 8, LANES), F32), pltpu.VMEM((2, 288, LANES), F32)],
        compiler_params=pltpu.CompilerParams(vmem_limit_bytes=8 << 20),
        cost_estimate=pl.CostEstimate(flops=1 << 18, bytes_accessed=1 << 18, transcendentals=0),
        name="regroup",
    )(turned)


def bands_kernel(filter_ref, out_ref, table):
    group = lane_ids(32) // 32
    zero = jnp.zeros((32, LANES), F32)

    def tap(t):
        return filter_ref[t].astype(F32) if 0 <= t < 64 else zero

    for m in range(72):
        block = tap(m)
        for jo in range(1, 4):
            block = jnp.where(group == jo, tap(m - jo), block)
        for part in range(2):
            at = 128 * (m // 4) + 2 * (m % 4) + part
            table[pl.ds(at, 16, stride=8), :] = block[16 * part : 16 * part + 16, :]
    out_ref[...] = table[...].astype(BF16)


def bands(filter_table):
    return pl.pallas_call(
        bands_kernel,
        out_shape=jax.ShapeDtypeStruct((2304, LANES), BF16),
        scratch_shapes=[pltpu.VMEM((2304, LANES), F32)],
        compiler_params=pltpu.CompilerParams(vmem_limit_bytes=8 << 20),
        cost_estimate=pl.CostEstimate(flops=1 << 20, bytes_accessed=1 << 20, transcendentals=0),
        name="bands",
    )(filter_table)


def migrate(quad, info_ref, pulse):
    rows = quad[0].shape[0]
    group = lane_ids(rows) // 32
    shifted = [quad]
    for f in range(1, 4):
        rolled = [pltpu.roll(q, LANES - 32 * f, 1) for q in quad]
        shifted.append([jnp.where(group < 4 - f, rolled[k], rolled[k + 1]) for k in range(3)])
    halves = []
    for half in range(2):
        first = info_ref[half : half + 1, :]
        width = info_ref[2 + half : 3 + half, :]
        low = info_ref[4 + half : 5 + half, :]
        high = info_ref[6 + half : 7 + half, :]
        total = jnp.zeros((rows, LANES), F32)
        for step in range(8):
            inside = (first <= step) & (step < first + width)
            total = total + jnp.where(inside, shifted[step % 4][half + step // 4], 0.0)
        total = total * (1.0 / width.astype(F32))
        halves.append(jnp.where((pulse >= low) & (pulse < high), total, 0.0))
    return halves


def azimuth_kernel(
    turned_ref, info_ref, bands_ref, out_ref, quads, field, pair, result, planes, final
):
    quads[...] = turned_ref[...].astype(F32)
    slot = lax.broadcasted_iota(jnp.int32, (24, LANES), 0)
    for core in range(2):
        pulse = 8 * slot + 4 * core + lane_ids(24) // 2 % 4
        halves = []
        for y in range(4):
            at = 96 * LAST.index((y, core))
            quad = [quads[pl.ds(at + k, 24, stride=4), :] for k in range(4)]
            halves.append(migrate(quad, info_ref, pulse))
        for half in range(2):
            for il, piece in enumerate(swap_blocks([h[half] for h in halves], 32)):
                field[pl.ds(8 * core + 4 * half + il, 24, stride=16), :] = piece
    field[384:392, :] = jnp.zeros((8, LANES), F32)
    pair[:, :LANES] = field[0:384, :].astype(BF16)
    pair[:, LANES:] = field[8:392, :].astype(BF16)
    total = jnp.zeros((256, LANES), F32)
    for e in range(9):
        total = total + jnp.dot(
            pair[16 * e : 16 * e + 256, :],
            bands_ref[256 * e : 256 * e + 256, :],
            preferred_element_type=F32,
        )
    result[...] = total
    for half in range(2):
        arrays = [result[pl.ds(4 * half + i, 32, stride=8), :] for i in range(4)]
        for jo, piece in enumerate(swap_blocks(arrays, 32)):
            planes[pl.ds(128 * half + jo, 32, stride=4), :] = piece
        turned = planes[128 * half : 128 * half + 128, :].T
        for i in range(4):
            final[pl.ds(4 * half + i, 32, stride=8), :] = turned[32 * i : 32 * i + 32, :]
    out_ref[...] = final[...].astype(BF16)


def azimuth(turned, info, band_matrix):
    return pl.pallas_call(
        azimuth_kernel,
        out_shape=jax.ShapeDtypeStruct((256, LANES), BF16),
        scratch_shapes=[
            pltpu.VMEM((768, LANES), F32),
            pltpu.VMEM((392, LANES), F32),
            pltpu.VMEM((384, 256), BF16),
            pltpu.VMEM((256, LANES), F32),
            pltpu.VMEM((256, LANES), F32),
            pltpu.VMEM((256, LANES), F32),
        ],
        cost_estimate=pl.CostEstimate(
            flops=2 * 256 * 128 * 2304, bytes_accessed=1 << 20, transcendentals=0
        ),
        compiler_params=pltpu.CompilerParams(vmem_limit_bytes=8 << 20),
        name="azimuth",
    )(turned, info, band_matrix)


def filter_table(recon_filters):
    real = recon_filters[:, :, 0].transpose(2, 1, 0)
    imag = recon_filters[:, :, 1].transpose(2, 1, 0)
    from_real = jnp.stack([real, imag], -1).reshape(64, 16, 32)
    from_imag = jnp.stack([-imag, real], -1).reshape(64, 16, 32)
    return jnp.tile(jnp.concatenate([from_real, from_imag], 1), (1, 1, 4))


def bin_info(span_offset, span_width, aperture_edges):
    origin = 128 * lax.axis_index("chan") - 32
    info = jnp.stack(
        [span_offset, span_width, aperture_edges[0] - origin, 512 - aperture_edges[1] - origin], 0
    )
    return jnp.repeat(info.reshape(8, 4), 32, axis=1)


def body(echoes, replica, recon_filters, span_offset, span_width, aperture_edges):
    chunks = compress(echoes, replica)
    order = [slot + i for _, slot, count in SEGMENTS for i in range(count)]
    turned = lax.all_to_all(chunks, "slot", 0, 0, tiled=True, axis_index_groups=[order])
    info = bin_info(span_offset, span_width, aperture_edges)
    band_matrix = bands(filter_table(recon_filters))
    windows = regroup(turned)
    gathered = lax.all_to_all(
        windows.reshape(8, 96, LANES),
        ("chan", "core"),
        0,
        0,
        tiled=True,
        axis_index_groups=[[2 * y + core for y, core in LAST]],
    )
    image = azimuth(gathered.reshape(768, LANES), info, band_matrix)
    return image.reshape(16, 2, 8, LANES)


def solution(mesh):
    split = Mesh(mesh.devices.reshape(64, 2, 4), ("slot", "core", "chan"))
    pulse = ("slot", "core")
    return jax.shard_map(
        body,
        mesh=split,
        in_specs=(
            P("chan", pulse, None, None),
            P(),
            P(),
            P(pulse),
            P(pulse),
            P(None, pulse),
        ),
        out_specs=P(None, None, pulse, "chan"),
        check_vma=False,
    )
```

```python
import jax
import jax.numpy as jnp
from jax import lax
from jax.experimental import pallas as pl
from jax.experimental.pallas import tpu as pltpu
from jax.sharding import Mesh
from jax.sharding import PartitionSpec as P

F32 = jnp.float32
BF16 = jnp.bfloat16
LANES = 128
NT = (((1,), (1,)), ((), ()))
FIRST = 41
LAST = ((2, 0), (2, 1), (3, 0), (3, 1), (0, 0), (0, 1), (1, 0), (1, 1))
SEGMENTS = ((0, FIRST, 64 - FIRST), (64 - FIRST, 0, FIRST))


def lane_ids(rows):
    return lax.broadcasted_iota(jnp.int32, (rows, LANES), 1)


def swap_blocks(arrays, width):
    arrays = list(arrays)
    group = lane_ids(arrays[0].shape[0]) // width
    bit = 1
    while bit < len(arrays):
        low = (group & bit) == 0
        shift = bit * width
        for first in range(len(arrays)):
            if first & bit:
                continue
            second = first | bit
            a, b = arrays[first], arrays[second]
            arrays[first] = jnp.where(low, a, pltpu.roll(b, shift, 1))
            arrays[second] = jnp.where(low, pltpu.roll(a, LANES - shift, 1), b)
        bit *= 2
    return arrays


def compress_kernel(
    echo_ref, replica_hbm, out_ref, replica_ref, echo_rows, sems, taps, windows, parts, rows, chunks
):
    taps_copy = pltpu.make_async_copy(replica_hbm, replica_ref, sems.at[16])
    taps_copy.start()
    copies = [
        pltpu.make_async_copy(
            echo_ref.at[row // 4, row % 4], echo_rows.at[pl.ds(2 * row, 2), :], sems.at[row]
        )
        for row in range(16)
    ]
    for copy in copies:
        copy.start()
    taps_copy.wait()
    lane = lane_ids(32)
    shift = 4 * lax.broadcasted_iota(jnp.int32, (32, LANES), 0)
    zero = jnp.zeros((32, LANES), F32)
    for part in range(2):
        previous = zero
        for m in range(33):
            if m < 32:
                row = replica_ref[part : part + 1, m * LANES : (m + 1) * LANES].astype(F32)
                rolled = pltpu.roll(
                    jnp.broadcast_to(row, (32, LANES)), 0, 1, stride=4, stride_axis=0
                )
            else:
                rolled = zero
            tile = jnp.where(lane >= shift, rolled, previous).astype(BF16)
            previous = rolled
            for a in range(4):
                taps[
                    part * 128 + 32 * a : part * 128 + 32 * a + 32,
                    (m + a) * LANES : (m + a + 1) * LANES,
                ] = tile
        for a in range(4):
            base = part * 128 + 32 * a
            if a:
                taps[base : base + 32, : a * LANES] = jnp.zeros((32, a * LANES), BF16)
            if a < 3:
                taps[base : base + 32, (33 + a) * LANES :] = jnp.zeros(
                    (32, (3 - a) * LANES), BF16
                )
    for copy in copies:
        copy.wait()
    for w in range(8):
        windows[32 * w : 32 * w + 32, :] = echo_rows[:, 512 * w : 512 * w + 4608]
    product = lax.dot_general(taps[...], windows[...], NT, preferred_element_type=F32)
    real_lane = lane_ids(128) % 2 == 0
    for half in range(2):
        by_real = product[:128, 128 * half : 128 * half + 128]
        by_imag = product[128:, 128 * half : 128 * half + 128]
        parts[128 * half : 128 * half + 128, :] = by_real + jnp.where(
            real_lane, -pltpu.roll(by_imag, LANES - 1, 1), pltpu.roll(by_imag, 1, 1)
        )
        pieces = [parts[pl.ds(128 * half + il, 32, stride=4), :] for il in range(4)]
        for w, piece in enumerate(swap_blocks(pieces, 32)):
            at = 128 * half + 32 * w
            rows[at : at + 32, :] = piece
    rows[256:264, :] = jnp.zeros((8, LANES), F32)
    for at, slot, count in SEGMENTS:
        for k in range(6):
            chunks[at : at + count, k, :] = rows[pl.ds(4 * slot + k, count, stride=4), :]
    out_ref[...] = chunks[:, 0:6, :].astype(BF16)


def compress(echoes, replica):
    return pl.pallas_call(
        compress_kernel,
        out_shape=jax.ShapeDtypeStruct((64, 6, LANES), BF16),
        in_specs=[
            pl.BlockSpec(memory_space=pltpu.HBM),
            pl.BlockSpec(memory_space=pltpu.HBM),
        ],
        scratch_shapes=[
            pltpu.VMEM((2, 4096), BF16),
            pltpu.VMEM((32, 8192), BF16),
            pltpu.SemaphoreType.DMA((17,)),
            pltpu.VMEM((256, 4608), BF16),
            pltpu.VMEM((256, 4608), BF16),
            pltpu.VMEM((256, LANES), F32),
            pltpu.VMEM((264, LANES), F32),
            pltpu.VMEM((64, 8, LANES), F32),
        ],
        compiler_params=pltpu.CompilerParams(vmem_limit_bytes=16 << 20),
        cost_estimate=pl.CostEstimate(
            flops=2 * 256 * 256 * 4608, bytes_accessed=1 << 20, transcendentals=0
        ),
        name="compress",
    )(
        pltpu.with_memory_space_constraint(echoes, pltpu.HBM),
        pltpu.with_memory_space_constraint(replica, pltpu.HBM),
    )


def regroup_kernel(turned_ref, out_ref, quads, rows):
    quads[:, 0:6, :] = turned_ref[...].astype(F32)
    for core in range(2):
        rows[core, 0:16, :] = jnp.zeros((16, LANES), F32)
        rows[core, 272:288, :] = jnp.zeros((16, LANES), F32)
        for at, slot, count in SEGMENTS:
            for k in range(4):
                rows[core, pl.ds(16 + 4 * slot + k, count, stride=4), :] = quads[
                    at : at + count, 2 * core + k, :
                ]
    for at, (y, core) in enumerate(LAST):
        out_ref[96 * at : 96 * at + 96, :] = rows[core, 64 * y : 64 * y + 96, :].astype(BF16)


def regroup(turned):
    return pl.pallas_call(
        regroup_kernel,
        out_shape=jax.ShapeDtypeStruct((768, LANES), BF16),
        scratch_shapes=[pltpu.VMEM((64, 8, LANES), F32), pltpu.VMEM((2, 288, LANES), F32)],
        compiler_params=pltpu.CompilerParams(vmem_limit_bytes=8 << 20),
        cost_estimate=pl.CostEstimate(flops=1 << 18, bytes_accessed=1 << 18, transcendentals=0),
        name="regroup",
    )(turned)


def bands_kernel(
    filter_ref, offset_ref, width_ref, edges_ref, out_ref, info_ref, spread, table
):
    group = lane_ids(32) // 32
    zero = jnp.zeros((32, LANES), F32)
    repeat = lane_ids(32) % 32 == lax.broadcasted_iota(jnp.int32, (32, LANES), 0)
    spread[...] = jnp.dot(
        filter_ref[...].reshape(2048, 32), repeat.astype(BF16), preferred_element_type=F32
    )

    def tap(t):
        return spread[32 * t : 32 * t + 32, :] if 0 <= t < 64 else zero

    for m in range(72):
        block = tap(m)
        for jo in range(1, 4):
            block = jnp.where(group == jo, tap(m - jo), block)
        for part in range(2):
            at = 128 * (m // 4) + 2 * (m % 4) + part
            table[pl.ds(at, 16, stride=8), :] = block[16 * part : 16 * part + 16, :]
    out_ref[...] = table[...].astype(BF16)

    def spread_bins(value):
        rows = []
        for half in range(2):
            row = jnp.full((1, LANES), value(4 * half), jnp.int32)
            for il in range(1, 4):
                row = jnp.where(group[:1] == il, value(4 * half + il), row)
            rows.append(row)
        return rows

    values = (
        lambda i: offset_ref[i],
        lambda i: width_ref[i],
        lambda i: edges_ref[0, i],
        lambda i: 512 - edges_ref[1, i],
    )
    for kind, value in enumerate(values):
        for half, row in enumerate(spread_bins(value)):
            info_ref[2 * kind + half : 2 * kind + half + 1, :] = row


def bands(filter_table, span_offset, span_width, aperture_edges):
    scalars = pl.BlockSpec(memory_space=pltpu.SMEM)
    return pl.pallas_call(
        bands_kernel,
        out_shape=(
            jax.ShapeDtypeStruct((2304, LANES), BF16),
            jax.ShapeDtypeStruct((8, LANES), jnp.int32),
        ),
        in_specs=[pl.BlockSpec(memory_space=pltpu.VMEM), scalars, scalars, scalars],
        scratch_shapes=[pltpu.VMEM((2048, LANES), F32), pltpu.VMEM((2304, LANES), F32)],
        compiler_params=pltpu.CompilerParams(vmem_limit_bytes=8 << 20),
        cost_estimate=pl.CostEstimate(flops=1 << 20, bytes_accessed=1 << 20, transcendentals=0),
        name="bands",
    )(filter_table, span_offset, span_width, aperture_edges)


def migrate(quad, info_ref, pulse):
    rows = quad[0].shape[0]
    group = lane_ids(rows) // 32
    shifted = [quad]
    for f in range(1, 4):
        rolled = [pltpu.roll(q, LANES - 32 * f, 1) for q in quad]
        shifted.append([jnp.where(group < 4 - f, rolled[k], rolled[k + 1]) for k in range(3)])
    halves = []
    for half in range(2):
        first = info_ref[half : half + 1, :]
        width = info_ref[2 + half : 3 + half, :]
        low = info_ref[4 + half : 5 + half, :]
        high = info_ref[6 + half : 7 + half, :]
        total = jnp.zeros((rows, LANES), F32)
        for step in range(8):
            inside = (first <= step) & (step < first + width)
            total = total + jnp.where(inside, shifted[step % 4][half + step // 4], 0.0)
        total = total * (1.0 / width.astype(F32))
        halves.append(jnp.where((pulse >= low) & (pulse < high), total, 0.0))
    return halves


def azimuth_kernel(
    turned_ref, info_ref, bands_ref, out_ref, quads, field, pair, result, planes, final
):
    quads[...] = turned_ref[...].astype(F32)
    slot = lax.broadcasted_iota(jnp.int32, (24, LANES), 0)
    origin = 128 * lax.axis_index("chan") - 32
    for core in range(2):
        pulse = origin + 8 * slot + 4 * core + lane_ids(24) // 2 % 4
        halves = []
        for y in range(4):
            at = 96 * LAST.index((y, core))
            quad = [quads[pl.ds(at + k, 24, stride=4), :] for k in range(4)]
            halves.append(migrate(quad, info_ref, pulse))
        for half in range(2):
            for il, piece in enumerate(swap_blocks([h[half] for h in halves], 32)):
                field[pl.ds(8 * core + 4 * half + il, 24, stride=16), :] = piece
    field[384:392, :] = jnp.zeros((8, LANES), F32)
    pair[:, :LANES] = field[0:384, :].astype(BF16)
    pair[:, LANES:] = field[8:392, :].astype(BF16)
    total = jnp.zeros((256, LANES), F32)
    for e in range(9):
        total = total + jnp.dot(
            pair[16 * e : 16 * e + 256, :],
            bands_ref[256 * e : 256 * e + 256, :],
            preferred_element_type=F32,
        )
    result[...] = total
    for half in range(2):
        arrays = [result[pl.ds(4 * half + i, 32, stride=8), :] for i in range(4)]
        for jo, piece in enumerate(swap_blocks(arrays, 32)):
            planes[pl.ds(128 * half + jo, 32, stride=4), :] = piece
        turned = planes[128 * half : 128 * half + 128, :].T
        for i in range(4):
            final[pl.ds(4 * half + i, 32, stride=8), :] = turned[32 * i : 32 * i + 32, :]
    out_ref[...] = final[...].astype(BF16)


def azimuth(turned, info, band_matrix):
    return pl.pallas_call(
        azimuth_kernel,
        out_shape=jax.ShapeDtypeStruct((256, LANES), BF16),
        scratch_shapes=[
            pltpu.VMEM((768, LANES), F32),
            pltpu.VMEM((392, LANES), F32),
            pltpu.VMEM((384, 256), BF16),
            pltpu.VMEM((256, LANES), F32),
            pltpu.VMEM((256, LANES), F32),
            pltpu.VMEM((256, LANES), F32),
        ],
        cost_estimate=pl.CostEstimate(
            flops=2 * 256 * 128 * 2304, bytes_accessed=1 << 20, transcendentals=0
        ),
        compiler_params=pltpu.CompilerParams(vmem_limit_bytes=8 << 20),
        name="azimuth",
    )(turned, info, band_matrix)


def filter_table(recon_filters):
    real = recon_filters[:, :, 0].transpose(2, 1, 0)
    imag = recon_filters[:, :, 1].transpose(2, 1, 0)
    from_real = jnp.stack([real, imag], -1).reshape(64, 16, 32)
    from_imag = jnp.stack([-imag, real], -1).reshape(64, 16, 32)
    return jnp.concatenate([from_real, from_imag], 1)


def body(echoes, replica, recon_filters, span_offset, span_width, aperture_edges):
    chunks = compress(echoes, replica)
    order = [slot + i for _, slot, count in SEGMENTS for i in range(count)]
    turned = lax.all_to_all(chunks, "slot", 0, 0, tiled=True, axis_index_groups=[order])
    windows = regroup(turned)
    windows, recon_filters, span_offset, span_width, aperture_edges = lax.optimization_barrier(
        (windows, recon_filters, span_offset, span_width, aperture_edges)
    )
    band_matrix, info = bands(
        filter_table(recon_filters), span_offset, span_width, aperture_edges
    )
    gathered = lax.all_to_all(
        windows.reshape(8, 96, LANES),
        ("chan", "core"),
        0,
        0,
        tiled=True,
        axis_index_groups=[[2 * y + core for y, core in LAST]],
    )
    image = azimuth(gathered.reshape(768, LANES), info, band_matrix)
    return image.reshape(16, 2, 8, LANES)


def solution(mesh):
    split = Mesh(mesh.devices.reshape(64, 2, 4), ("slot", "core", "chan"))
    pulse = ("slot", "core")
    return jax.shard_map(
        body,
        mesh=split,
        in_specs=(
            P("chan", pulse, None, None),
            P(),
            P(),
            P(pulse),
            P(pulse),
            P(None, pulse),
        ),
        out_specs=P(None, None, pulse, "chan"),
        check_vma=False,
    )
```

```python
import jax
import jax.numpy as jnp
from jax import lax
from jax.experimental import pallas as pl
from jax.experimental.pallas import tpu as pltpu
from jax.sharding import Mesh
from jax.sharding import PartitionSpec as P

F32 = jnp.float32
BF16 = jnp.bfloat16
LANES = 128
NT = (((1,), (1,)), ((), ()))
FIRST = 41
LAST = ((2, 1), (2, 0), (3, 1), (3, 0), (0, 1), (0, 0), (1, 1), (1, 0))
SEGMENTS = ((0, FIRST, 64 - FIRST), (64 - FIRST, 0, FIRST))


def lane_ids(rows):
    return lax.broadcasted_iota(jnp.int32, (rows, LANES), 1)


def swap_blocks(arrays, width):
    arrays = list(arrays)
    group = lane_ids(arrays[0].shape[0]) // width
    bit = 1
    while bit < len(arrays):
        low = (group & bit) == 0
        shift = bit * width
        for first in range(len(arrays)):
            if first & bit:
                continue
            second = first | bit
            a, b = arrays[first], arrays[second]
            arrays[first] = jnp.where(low, a, pltpu.roll(b, shift, 1))
            arrays[second] = jnp.where(low, pltpu.roll(a, LANES - shift, 1), b)
        bit *= 2
    return arrays


def compress_kernel(
    echo_ref, replica_hbm, out_ref, replica_ref, echo_rows, sems, taps, windows, parts, rows, chunks
):
    taps_copy = pltpu.make_async_copy(replica_hbm, replica_ref, sems.at[16])
    taps_copy.start()
    copies = [
        pltpu.make_async_copy(
            echo_ref.at[row // 4, row % 4], echo_rows.at[pl.ds(2 * row, 2), :], sems.at[row]
        )
        for row in range(16)
    ]
    for copy in copies:
        copy.start()
    taps_copy.wait()
    lane = lane_ids(32)
    shift = 4 * lax.broadcasted_iota(jnp.int32, (32, LANES), 0)
    zero = jnp.zeros((32, LANES), F32)
    for part in range(2):
        previous = zero
        for m in range(33):
            if m < 32:
                row = replica_ref[part : part + 1, m * LANES : (m + 1) * LANES].astype(F32)
                rolled = pltpu.roll(
                    jnp.broadcast_to(row, (32, LANES)), 0, 1, stride=4, stride_axis=0
                )
            else:
                rolled = zero
            tile = jnp.where(lane >= shift, rolled, previous).astype(BF16)
            previous = rolled
            for a in range(4):
                taps[
                    part * 128 + 32 * a : part * 128 + 32 * a + 32,
                    (m + a) * LANES : (m + a + 1) * LANES,
                ] = tile
        for a in range(4):
            base = part * 128 + 32 * a
            if a:
                taps[base : base + 32, : a * LANES] = jnp.zeros((32, a * LANES), BF16)
            if a < 3:
                taps[base : base + 32, (33 + a) * LANES :] = jnp.zeros(
                    (32, (3 - a) * LANES), BF16
                )
    for copy in copies:
        copy.wait()
    for w in range(8):
        windows[32 * w : 32 * w + 32, :] = echo_rows[:, 512 * w : 512 * w + 4608]
    product = lax.dot_general(taps[...], windows[...], NT, preferred_element_type=F32)
    real_lane = lane_ids(128) % 2 == 0
    for half in range(2):
        by_real = product[:128, 128 * half : 128 * half + 128]
        by_imag = product[128:, 128 * half : 128 * half + 128]
        parts[128 * half : 128 * half + 128, :] = by_real + jnp.where(
            real_lane, -pltpu.roll(by_imag, LANES - 1, 1), pltpu.roll(by_imag, 1, 1)
        )
        pieces = [parts[pl.ds(128 * half + il, 32, stride=4), :] for il in range(4)]
        for w, piece in enumerate(swap_blocks(pieces, 32)):
            at = 128 * half + 32 * w
            rows[at : at + 32, :] = piece
    rows[256:264, :] = jnp.zeros((8, LANES), F32)
    for at, slot, count in SEGMENTS:
        for k in range(6):
            chunks[at : at + count, k, :] = rows[pl.ds(4 * slot + k, count, stride=4), :]
    out_ref[...] = chunks[:, 0:6, :].astype(BF16)


def compress(echoes, replica):
    return pl.pallas_call(
        compress_kernel,
        out_shape=jax.ShapeDtypeStruct((64, 6, LANES), BF16),
        in_specs=[
            pl.BlockSpec(memory_space=pltpu.HBM),
            pl.BlockSpec(memory_space=pltpu.HBM),
        ],
        scratch_shapes=[
            pltpu.VMEM((2, 4096), BF16),
            pltpu.VMEM((32, 8192), BF16),
            pltpu.SemaphoreType.DMA((17,)),
            pltpu.VMEM((256, 4608), BF16),
            pltpu.VMEM((256, 4608), BF16),
            pltpu.VMEM((256, LANES), F32),
            pltpu.VMEM((264, LANES), F32),
            pltpu.VMEM((64, 8, LANES), F32),
        ],
        compiler_params=pltpu.CompilerParams(vmem_limit_bytes=16 << 20),
        cost_estimate=pl.CostEstimate(
            flops=2 * 256 * 256 * 4608, bytes_accessed=1 << 20, transcendentals=0
        ),
        name="compress",
    )(
        pltpu.with_memory_space_constraint(echoes, pltpu.HBM),
        pltpu.with_memory_space_constraint(replica, pltpu.HBM),
    )


def regroup_kernel(turned_ref, out_ref, quads, rows):
    quads[:, 0:6, :] = turned_ref[...].astype(F32)
    for core in range(2):
        rows[core, 0:16, :] = jnp.zeros((16, LANES), F32)
        rows[core, 272:288, :] = jnp.zeros((16, LANES), F32)
        for at, slot, count in SEGMENTS:
            for k in range(4):
                rows[core, pl.ds(16 + 4 * slot + k, count, stride=4), :] = quads[
                    at : at + count, 2 * core + k, :
                ]
    for at, (y, core) in enumerate(LAST):
        out_ref[96 * at : 96 * at + 96, :] = rows[core, 64 * y : 64 * y + 96, :].astype(BF16)


def regroup(turned):
    return pl.pallas_call(
        regroup_kernel,
        out_shape=jax.ShapeDtypeStruct((768, LANES), BF16),
        scratch_shapes=[pltpu.VMEM((64, 8, LANES), F32), pltpu.VMEM((2, 288, LANES), F32)],
        compiler_params=pltpu.CompilerParams(vmem_limit_bytes=8 << 20),
        cost_estimate=pl.CostEstimate(flops=1 << 18, bytes_accessed=1 << 18, transcendentals=0),
        name="regroup",
    )(turned)


def bands_kernel(
    filter_ref, offset_ref, width_ref, edges_ref, out_ref, info_ref, spread, table
):
    group = lane_ids(32) // 32
    zero = jnp.zeros((32, LANES), F32)
    repeat = lane_ids(32) % 32 == lax.broadcasted_iota(jnp.int32, (32, LANES), 0)
    spread[...] = jnp.dot(
        filter_ref[...].reshape(2048, 32), repeat.astype(BF16), preferred_element_type=F32
    )

    def tap(t):
        return spread[32 * t : 32 * t + 32, :] if 0 <= t < 64 else zero

    for m in range(72):
        block = tap(m)
        for jo in range(1, 4):
            block = jnp.where(group == jo, tap(m - jo), block)
        for part in range(2):
            at = 128 * (m // 4) + 2 * (m % 4) + part
            table[pl.ds(at, 16, stride=8), :] = block[16 * part : 16 * part + 16, :]
    out_ref[...] = table[...].astype(BF16)

    def spread_bins(value):
        rows = []
        for half in range(2):
            row = jnp.full((1, LANES), value(4 * half), jnp.int32)
            for il in range(1, 4):
                row = jnp.where(group[:1] == il, value(4 * half + il), row)
            rows.append(row)
        return rows

    values = (
        lambda i: offset_ref[i],
        lambda i: width_ref[i],
        lambda i: edges_ref[0, i],
        lambda i: 512 - edges_ref[1, i],
    )
    for kind, value in enumerate(values):
        for half, row in enumerate(spread_bins(value)):
            info_ref[2 * kind + half : 2 * kind + half + 1, :] = row


def bands(filter_table, span_offset, span_width, aperture_edges):
    scalars = pl.BlockSpec(memory_space=pltpu.SMEM)
    return pl.pallas_call(
        bands_kernel,
        out_shape=(
            jax.ShapeDtypeStruct((2304, LANES), BF16),
            jax.ShapeDtypeStruct((8, LANES), jnp.int32),
        ),
        in_specs=[pl.BlockSpec(memory_space=pltpu.VMEM), scalars, scalars, scalars],
        scratch_shapes=[pltpu.VMEM((2048, LANES), F32), pltpu.VMEM((2304, LANES), F32)],
        compiler_params=pltpu.CompilerParams(vmem_limit_bytes=8 << 20),
        cost_estimate=pl.CostEstimate(flops=1 << 20, bytes_accessed=1 << 20, transcendentals=0),
        name="bands",
    )(filter_table, span_offset, span_width, aperture_edges)


def migrate(quad, info_ref, pulse):
    rows = quad[0].shape[0]
    group = lane_ids(rows) // 32
    shifted = [quad]
    for f in range(1, 4):
        rolled = [pltpu.roll(q, LANES - 32 * f, 1) for q in quad]
        shifted.append([jnp.where(group < 4 - f, rolled[k], rolled[k + 1]) for k in range(3)])
    halves = []
    for half in range(2):
        first = info_ref[half : half + 1, :]
        width = info_ref[2 + half : 3 + half, :]
        low = info_ref[4 + half : 5 + half, :]
        high = info_ref[6 + half : 7 + half, :]
        total = jnp.zeros((rows, LANES), F32)
        for step in range(8):
            inside = (first <= step) & (step < first + width)
            total = total + jnp.where(inside, shifted[step % 4][half + step // 4], 0.0)
        total = total * (1.0 / width.astype(F32))
        halves.append(jnp.where((pulse >= low) & (pulse < high), total, 0.0))
    return halves


def azimuth_kernel(
    turned_ref, info_ref, bands_ref, out_ref, quads, field, pair, result, planes, final
):
    quads[...] = turned_ref[...].astype(F32)
    slot = lax.broadcasted_iota(jnp.int32, (24, LANES), 0)
    origin = 128 * lax.axis_index("chan") - 32
    for core in range(2):
        pulse = origin + 8 * slot + 4 * core + lane_ids(24) // 2 % 4
        halves = []
        for y in range(4):
            at = 96 * LAST.index((y, core))
            quad = [quads[pl.ds(at + k, 24, stride=4), :] for k in range(4)]
            halves.append(migrate(quad, info_ref, pulse))
        for half in range(2):
            for il, piece in enumerate(swap_blocks([h[half] for h in halves], 32)):
                field[pl.ds(8 * core + 4 * half + il, 24, stride=16), :] = piece
    field[384:392, :] = jnp.zeros((8, LANES), F32)
    pair[:, :LANES] = field[0:384, :].astype(BF16)
    pair[:, LANES:] = field[8:392, :].astype(BF16)
    total = jnp.zeros((256, LANES), F32)
    for e in range(9):
        total = total + jnp.dot(
            pair[16 * e : 16 * e + 256, :],
            bands_ref[256 * e : 256 * e + 256, :],
            preferred_element_type=F32,
        )
    result[...] = total
    for half in range(2):
        arrays = [result[pl.ds(4 * half + i, 32, stride=8), :] for i in range(4)]
        for jo, piece in enumerate(swap_blocks(arrays, 32)):
            planes[pl.ds(128 * half + jo, 32, stride=4), :] = piece
        turned = planes[128 * half : 128 * half + 128, :].T
        for i in range(4):
            final[pl.ds(4 * half + i, 32, stride=8), :] = turned[32 * i : 32 * i + 32, :]
    out_ref[...] = final[...].astype(BF16)


def azimuth(turned, info, band_matrix):
    return pl.pallas_call(
        azimuth_kernel,
        out_shape=jax.ShapeDtypeStruct((256, LANES), BF16),
        scratch_shapes=[
            pltpu.VMEM((768, LANES), F32),
            pltpu.VMEM((392, LANES), F32),
            pltpu.VMEM((384, 256), BF16),
            pltpu.VMEM((256, LANES), F32),
            pltpu.VMEM((256, LANES), F32),
            pltpu.VMEM((256, LANES), F32),
        ],
        cost_estimate=pl.CostEstimate(
            flops=2 * 256 * 128 * 2304, bytes_accessed=1 << 20, transcendentals=0
        ),
        compiler_params=pltpu.CompilerParams(vmem_limit_bytes=8 << 20),
        name="azimuth",
    )(turned, info, band_matrix)


def filter_table(recon_filters):
    real = recon_filters[:, :, 0].transpose(2, 1, 0)
    imag = recon_filters[:, :, 1].transpose(2, 1, 0)
    from_real = jnp.stack([real, imag], -1).reshape(64, 16, 32)
    from_imag = jnp.stack([-imag, real], -1).reshape(64, 16, 32)
    return jnp.concatenate([from_real, from_imag], 1)


def body(echoes, replica, recon_filters, span_offset, span_width, aperture_edges):
    chunks = compress(echoes, replica)
    order = [slot + i for _, slot, count in SEGMENTS for i in range(count)]
    turned = lax.all_to_all(chunks, "slot", 0, 0, tiled=True, axis_index_groups=[order])
    windows = regroup(turned)
    windows, recon_filters, span_offset, span_width, aperture_edges = lax.optimization_barrier(
        (windows, recon_filters, span_offset, span_width, aperture_edges)
    )
    band_matrix, info = bands(
        filter_table(recon_filters), span_offset, span_width, aperture_edges
    )
    gathered = lax.all_to_all(
        windows.reshape(8, 96, LANES),
        ("chan", "core"),
        0,
        0,
        tiled=True,
        axis_index_groups=[[2 * y + core for y, core in LAST]],
    )
    image = azimuth(gathered.reshape(768, LANES), info, band_matrix)
    return image.reshape(16, 2, 8, LANES)


def solution(mesh):
    split = Mesh(mesh.devices.reshape(64, 2, 4), ("slot", "core", "chan"))
    pulse = ("slot", "core")
    return jax.shard_map(
        body,
        mesh=split,
        in_specs=(
            P("chan", pulse, None, None),
            P(),
            P(),
            P(pulse),
            P(pulse),
            P(None, pulse),
        ),
        out_specs=P(None, None, pulse, "chan"),
        check_vma=False,
    )
```

```python
import jax
import jax.numpy as jnp
from jax import lax
from jax.experimental import pallas as pl
from jax.experimental.pallas import tpu as pltpu
from jax.sharding import Mesh
from jax.sharding import PartitionSpec as P

F32 = jnp.float32
BF16 = jnp.bfloat16
LANES = 128
NT = (((1,), (1,)), ((), ()))
FIRST = 40
LAST = ((2, 1), (2, 0), (3, 1), (3, 0), (0, 1), (0, 0), (1, 1), (1, 0))
SEGMENTS = ((0, FIRST, 64 - FIRST), (64 - FIRST, 0, FIRST))


def lane_ids(rows):
    return lax.broadcasted_iota(jnp.int32, (rows, LANES), 1)


def swap_blocks(arrays, width):
    arrays = list(arrays)
    group = lane_ids(arrays[0].shape[0]) // width
    bit = 1
    while bit < len(arrays):
        low = (group & bit) == 0
        shift = bit * width
        for first in range(len(arrays)):
            if first & bit:
                continue
            second = first | bit
            a, b = arrays[first], arrays[second]
            arrays[first] = jnp.where(low, a, pltpu.roll(b, shift, 1))
            arrays[second] = jnp.where(low, pltpu.roll(a, LANES - shift, 1), b)
        bit *= 2
    return arrays


def compress_kernel(
    echo_ref, replica_hbm, out_ref, replica_ref, echo_rows, sems, taps, windows, parts, rows, chunks
):
    taps_copy = pltpu.make_async_copy(replica_hbm, replica_ref, sems.at[16])
    taps_copy.start()
    copies = [
        pltpu.make_async_copy(
            echo_ref.at[row // 4, row % 4], echo_rows.at[pl.ds(2 * row, 2), :], sems.at[row]
        )
        for row in range(16)
    ]
    for copy in copies:
        copy.start()
    taps_copy.wait()
    lane = lane_ids(32)
    shift = 4 * lax.broadcasted_iota(jnp.int32, (32, LANES), 0)
    zero = jnp.zeros((32, LANES), F32)
    for part in range(2):
        previous = zero
        for m in range(33):
            if m < 32:
                row = replica_ref[part : part + 1, m * LANES : (m + 1) * LANES].astype(F32)
                rolled = pltpu.roll(
                    jnp.broadcast_to(row, (32, LANES)), 0, 1, stride=4, stride_axis=0
                )
            else:
                rolled = zero
            tile = jnp.where(lane >= shift, rolled, previous).astype(BF16)
            previous = rolled
            for a in range(4):
                taps[
                    part * 128 + 32 * a : part * 128 + 32 * a + 32,
                    (m + a) * LANES : (m + a + 1) * LANES,
                ] = tile
        for a in range(4):
            base = part * 128 + 32 * a
            if a:
                taps[base : base + 32, : a * LANES] = jnp.zeros((32, a * LANES), BF16)
            if a < 3:
                taps[base : base + 32, (33 + a) * LANES :] = jnp.zeros(
                    (32, (3 - a) * LANES), BF16
                )
    for copy in copies:
        copy.wait()
    for w in range(8):
        windows[32 * w : 32 * w + 32, :] = echo_rows[:, 512 * w : 512 * w + 4608]
    product = lax.dot_general(taps[...], windows[...], NT, preferred_element_type=F32)
    real_lane = lane_ids(128) % 2 == 0
    for half in range(2):
        by_real = product[:128, 128 * half : 128 * half + 128]
        by_imag = product[128:, 128 * half : 128 * half + 128]
        parts[128 * half : 128 * half + 128, :] = by_real + jnp.where(
            real_lane, -pltpu.roll(by_imag, LANES - 1, 1), pltpu.roll(by_imag, 1, 1)
        )
        pieces = [parts[pl.ds(128 * half + il, 32, stride=4), :] for il in range(4)]
        for w, piece in enumerate(swap_blocks(pieces, 32)):
            at = 128 * half + 32 * w
            rows[at : at + 32, :] = piece
    rows[256:264, :] = jnp.zeros((8, LANES), F32)
    for at, slot, count in SEGMENTS:
        for k in range(6):
            chunks[at : at + count, k, :] = rows[pl.ds(4 * slot + k, count, stride=4), :]
    out_ref[...] = chunks[:, 0:6, :].astype(BF16)


def compress(echoes, replica):
    return pl.pallas_call(
        compress_kernel,
        out_shape=jax.ShapeDtypeStruct((64, 6, LANES), BF16),
        in_specs=[
            pl.BlockSpec(memory_space=pltpu.HBM),
            pl.BlockSpec(memory_space=pltpu.HBM),
        ],
        scratch_shapes=[
            pltpu.VMEM((2, 4096), BF16),
            pltpu.VMEM((32, 8192), BF16),
            pltpu.SemaphoreType.DMA((17,)),
            pltpu.VMEM((256, 4608), BF16),
            pltpu.VMEM((256, 4608), BF16),
            pltpu.VMEM((256, LANES), F32),
            pltpu.VMEM((264, LANES), F32),
            pltpu.VMEM((64, 8, LANES), F32),
        ],
        compiler_params=pltpu.CompilerParams(vmem_limit_bytes=16 << 20),
        cost_estimate=pl.CostEstimate(
            flops=2 * 256 * 256 * 4608, bytes_accessed=1 << 20, transcendentals=0
        ),
        name="compress",
    )(
        pltpu.with_memory_space_constraint(echoes, pltpu.HBM),
        pltpu.with_memory_space_constraint(replica, pltpu.HBM),
    )


def migrate(quad, info, pulse):
    rows = quad[0].shape[0]
    group = lane_ids(rows) // 32
    shifted = [quad]
    for f in range(1, 4):
        rolled = [pltpu.roll(q, LANES - 32 * f, 1) for q in quad]
        shifted.append([jnp.where(group < 4 - f, rolled[k], rolled[k + 1]) for k in range(3)])
    halves = []
    for half in range(2):
        first = info[half : half + 1, :]
        width = info[2 + half : 3 + half, :]
        low = info[4 + half : 5 + half, :]
        high = info[6 + half : 7 + half, :]
        total = jnp.zeros((rows, LANES), F32)
        for step in range(8):
            inside = (first <= step) & (step < first + width)
            total = total + jnp.where(inside, shifted[step % 4][half + step // 4], 0.0)
        total = total * (1.0 / width.astype(F32))
        halves.append(jnp.where((pulse >= low) & (pulse < high), total, 0.0))
    return halves


def regroup_kernel(turned_ref, info_ref, other_ref, out_ref, quads, rows):
    quads[:, 0:6, :] = turned_ref[...].astype(F32)
    here = lax.axis_index("core")
    slot = (lax.broadcasted_iota(jnp.int32, (64, LANES), 0) + FIRST) % 64
    pulse = 8 * slot + 4 * here + lane_ids(64) // 2 % 4
    for core in range(2):
        info = jnp.where(here == core, info_ref[...], other_ref[...])
        rows[core, 0:8, :] = jnp.zeros((8, LANES), F32)
        rows[core, 136:144, :] = jnp.zeros((8, LANES), F32)
        quad = [quads[:, 2 * core + k, :] for k in range(4)]
        for half, bins in enumerate(migrate(quad, info, pulse)):
            for at, first, count in SEGMENTS:
                rows[core, pl.ds(8 + 2 * first + half, count, stride=2), :] = bins[at : at + count]
    for at, (y, core) in enumerate(LAST):
        out_ref[48 * at : 48 * at + 48, :] = rows[core, 32 * y : 32 * y + 48, :].astype(BF16)


def regroup(turned, info, other):
    return pl.pallas_call(
        regroup_kernel,
        out_shape=jax.ShapeDtypeStruct((384, LANES), BF16),
        scratch_shapes=[pltpu.VMEM((64, 8, LANES), F32), pltpu.VMEM((2, 144, LANES), F32)],
        compiler_params=pltpu.CompilerParams(vmem_limit_bytes=8 << 20),
        cost_estimate=pl.CostEstimate(flops=1 << 20, bytes_accessed=1 << 18, transcendentals=0),
        name="regroup",
    )(turned, info, other)


def bands_kernel(
    filter_ref, offset_ref, width_ref, edges_ref, out_ref, info_ref, spread, table
):
    group = lane_ids(32) // 32
    zero = jnp.zeros((32, LANES), F32)
    repeat = lane_ids(32) % 32 == lax.broadcasted_iota(jnp.int32, (32, LANES), 0)
    spread[...] = jnp.dot(
        filter_ref[...].reshape(2048, 32), repeat.astype(BF16), preferred_element_type=F32
    )

    def tap(t):
        return spread[32 * t : 32 * t + 32, :] if 0 <= t < 64 else zero

    for m in range(72):
        block = tap(m)
        for jo in range(1, 4):
            block = jnp.where(group == jo, tap(m - jo), block)
        for part in range(2):
            at = 128 * (m // 4) + 2 * (m % 4) + part
            table[pl.ds(at, 16, stride=8), :] = block[16 * part : 16 * part + 16, :]
    out_ref[...] = table[...].astype(BF16)

    def spread_bins(value):
        rows = []
        for half in range(2):
            row = jnp.full((1, LANES), value(4 * half), jnp.int32)
            for il in range(1, 4):
                row = jnp.where(group[:1] == il, value(4 * half + il), row)
            rows.append(row)
        return rows

    values = (
        lambda i: offset_ref[i],
        lambda i: width_ref[i],
        lambda i: edges_ref[0, i],
        lambda i: 512 - edges_ref[1, i],
    )
    for kind, value in enumerate(values):
        for half, row in enumerate(spread_bins(value)):
            info_ref[2 * kind + half : 2 * kind + half + 1, :] = row


def bands(filter_table, span_offset, span_width, aperture_edges):
    scalars = pl.BlockSpec(memory_space=pltpu.SMEM)
    return pl.pallas_call(
        bands_kernel,
        out_shape=(
            jax.ShapeDtypeStruct((2304, LANES), BF16),
            jax.ShapeDtypeStruct((8, LANES), jnp.int32),
        ),
        in_specs=[pl.BlockSpec(memory_space=pltpu.VMEM), scalars, scalars, scalars],
        scratch_shapes=[pltpu.VMEM((2048, LANES), F32), pltpu.VMEM((2304, LANES), F32)],
        compiler_params=pltpu.CompilerParams(vmem_limit_bytes=8 << 20),
        cost_estimate=pl.CostEstimate(flops=1 << 20, bytes_accessed=1 << 20, transcendentals=0),
        name="bands",
    )(filter_table, span_offset, span_width, aperture_edges)


def azimuth_kernel(turned_ref, bands_ref, out_ref, bins, field, pair, result, planes, final):
    bins[...] = turned_ref[...].astype(F32)
    for core in range(2):
        for half in range(2):
            arrays = [
                bins[pl.ds(48 * LAST.index((y, core)) + half, 24, stride=2), :] for y in range(4)
            ]
            for il, piece in enumerate(swap_blocks(arrays, 32)):
                field[pl.ds(8 * core + 4 * half + il, 24, stride=16), :] = piece
    field[384:392, :] = jnp.zeros((8, LANES), F32)
    pair[:, :LANES] = field[0:384, :].astype(BF16)
    pair[:, LANES:] = field[8:392, :].astype(BF16)
    total = jnp.zeros((256, LANES), F32)
    for e in range(9):
        total = total + jnp.dot(
            pair[16 * e : 16 * e + 256, :],
            bands_ref[256 * e : 256 * e + 256, :],
            preferred_element_type=F32,
        )
    result[...] = total
    for half in range(2):
        arrays = [result[pl.ds(4 * half + i, 32, stride=8), :] for i in range(4)]
        for jo, piece in enumerate(swap_blocks(arrays, 32)):
            planes[pl.ds(128 * half + jo, 32, stride=4), :] = piece
        turned = planes[128 * half : 128 * half + 128, :].T
        for i in range(4):
            final[pl.ds(4 * half + i, 32, stride=8), :] = turned[32 * i : 32 * i + 32, :]
    out_ref[...] = final[...].astype(BF16)


def azimuth(turned, band_matrix):
    return pl.pallas_call(
        azimuth_kernel,
        out_shape=jax.ShapeDtypeStruct((256, LANES), BF16),
        scratch_shapes=[
            pltpu.VMEM((384, LANES), F32),
            pltpu.VMEM((392, LANES), F32),
            pltpu.VMEM((384, 256), BF16),
            pltpu.VMEM((256, LANES), F32),
            pltpu.VMEM((256, LANES), F32),
            pltpu.VMEM((256, LANES), F32),
        ],
        cost_estimate=pl.CostEstimate(
            flops=2 * 256 * 128 * 2304, bytes_accessed=1 << 20, transcendentals=0
        ),
        compiler_params=pltpu.CompilerParams(vmem_limit_bytes=8 << 20),
        name="azimuth",
    )(turned, band_matrix)


def filter_table(recon_filters):
    real = recon_filters[:, :, 0].transpose(2, 1, 0)
    imag = recon_filters[:, :, 1].transpose(2, 1, 0)
    from_real = jnp.stack([real, imag], -1).reshape(64, 16, 32)
    from_imag = jnp.stack([-imag, real], -1).reshape(64, 16, 32)
    return jnp.concatenate([from_real, from_imag], 1)


def body(echoes, replica, recon_filters, span_offset, span_width, aperture_edges):
    chunks = compress(echoes, replica)
    order = [slot + i for _, slot, count in SEGMENTS for i in range(count)]
    turned = lax.all_to_all(chunks, "slot", 0, 0, tiled=True, axis_index_groups=[order])
    _, recon_filters, span_offset, span_width, aperture_edges = lax.optimization_barrier(
        (chunks, recon_filters, span_offset, span_width, aperture_edges)
    )
    band_matrix, info = bands(
        filter_table(recon_filters), span_offset, span_width, aperture_edges
    )
    other = lax.ppermute(info, "core", [(0, 1), (1, 0)])
    windows = regroup(turned, info, other)
    gathered = lax.all_to_all(
        windows.reshape(8, 48, LANES),
        ("chan", "core"),
        0,
        0,
        tiled=True,
        axis_index_groups=[[2 * y + core for y, core in LAST]],
    )
    image = azimuth(gathered.reshape(384, LANES), band_matrix)
    return image.reshape(16, 2, 8, LANES)


def solution(mesh):
    split = Mesh(mesh.devices.reshape(64, 2, 4), ("slot", "core", "chan"))
    pulse = ("slot", "core")
    return jax.shard_map(
        body,
        mesh=split,
        in_specs=(
            P("chan", pulse, None, None),
            P(),
            P(),
            P(pulse),
            P(pulse),
            P(None, pulse),
        ),
        out_specs=P(None, None, pulse, "chan"),
        check_vma=False,
    )
```

```python
import jax
import jax.numpy as jnp
from jax import lax
from jax.experimental import pallas as pl
from jax.experimental.pallas import tpu as pltpu
from jax.sharding import Mesh
from jax.sharding import PartitionSpec as P

F32 = jnp.float32
BF16 = jnp.bfloat16
LANES = 128
NT = (((1,), (1,)), ((), ()))
FIRST = 40
LAST = ((2, 1), (2, 0), (3, 1), (3, 0), (0, 1), (0, 0), (1, 1), (1, 0))
SEGMENTS = ((0, FIRST, 64 - FIRST), (64 - FIRST, 0, FIRST))


def lane_ids(rows):
    return lax.broadcasted_iota(jnp.int32, (rows, LANES), 1)


def swap_blocks(arrays, width):
    arrays = list(arrays)
    group = lane_ids(arrays[0].shape[0]) // width
    bit = 1
    while bit < len(arrays):
        low = (group & bit) == 0
        shift = bit * width
        for first in range(len(arrays)):
            if first & bit:
                continue
            second = first | bit
            a, b = arrays[first], arrays[second]
            arrays[first] = jnp.where(low, a, pltpu.roll(b, shift, 1))
            arrays[second] = jnp.where(low, pltpu.roll(a, LANES - shift, 1), b)
        bit *= 2
    return arrays


def compress_kernel(
    echo_ref, replica_hbm, out_ref, replica_ref, echo_rows, sems, taps, windows, parts, rows, chunks, packed
):
    taps_copy = pltpu.make_async_copy(replica_hbm, replica_ref, sems.at[16])
    taps_copy.start()
    copies = [
        pltpu.make_async_copy(
            echo_ref.at[row // 4, row % 4], echo_rows.at[pl.ds(2 * row, 2), :], sems.at[row]
        )
        for row in range(16)
    ]
    for copy in copies:
        copy.start()
    taps_copy.wait()
    lane = lane_ids(32)
    shift = 4 * lax.broadcasted_iota(jnp.int32, (32, LANES), 0)
    zero = jnp.zeros((32, LANES), F32)
    for part in range(2):
        previous = zero
        for m in range(33):
            if m < 32:
                row = replica_ref[part : part + 1, m * LANES : (m + 1) * LANES].astype(F32)
                rolled = pltpu.roll(
                    jnp.broadcast_to(row, (32, LANES)), 0, 1, stride=4, stride_axis=0
                )
            else:
                rolled = zero
            tile = jnp.where(lane >= shift, rolled, previous).astype(BF16)
            previous = rolled
            for a in range(4):
                taps[
                    part * 128 + 32 * a : part * 128 + 32 * a + 32,
                    (m + a) * LANES : (m + a + 1) * LANES,
                ] = tile
        for a in range(4):
            base = part * 128 + 32 * a
            if a:
                taps[base : base + 32, : a * LANES] = jnp.zeros((32, a * LANES), BF16)
            if a < 3:
                taps[base : base + 32, (33 + a) * LANES :] = jnp.zeros(
                    (32, (3 - a) * LANES), BF16
                )
    for copy in copies:
        copy.wait()
    for w in range(8):
        windows[32 * w : 32 * w + 32, :] = echo_rows[:, 512 * w : 512 * w + 4608]
    product = lax.dot_general(taps[...], windows[...], NT, preferred_element_type=F32)
    out_copies = []
    real_lane = lane_ids(128) % 2 == 0
    for half in range(2):
        by_real = product[:128, 128 * half : 128 * half + 128]
        by_imag = product[128:, 128 * half : 128 * half + 128]
        parts[128 * half : 128 * half + 128, :] = by_real + jnp.where(
            real_lane, -pltpu.roll(by_imag, LANES - 1, 1), pltpu.roll(by_imag, 1, 1)
        )
        pieces = [parts[pl.ds(128 * half + il, 32, stride=4), :] for il in range(4)]
        for w, piece in enumerate(swap_blocks(pieces, 32)):
            at = 128 * half + 32 * w
            rows[at : at + 32, :] = piece
        if half == 0:
            rows[256:264, :] = jnp.zeros((8, LANES), F32)
        for at, slot, count in ((64 - FIRST, 0, 24),) if half == 0 else (
            (0, FIRST, 64 - FIRST),
            (88 - FIRST, 24, FIRST - 24),
        ):
            for k in range(6):
                chunks[at : at + count, k, :] = rows[pl.ds(4 * slot + k, count, stride=4), :]
            packed[at : at + count] = chunks[at : at + count, 0:6, :].astype(BF16)
            out_copies.append(
                pltpu.make_async_copy(
                    packed.at[pl.ds(at, count)], out_ref.at[pl.ds(at, count)], sems.at[at // 8]
                )
            )
            out_copies[-1].start()
    for copy in out_copies:
        copy.wait()


def compress(echoes, replica):
    return pl.pallas_call(
        compress_kernel,
        out_shape=jax.ShapeDtypeStruct((64, 6, LANES), BF16),
        in_specs=[
            pl.BlockSpec(memory_space=pltpu.HBM),
            pl.BlockSpec(memory_space=pltpu.HBM),
        ],
        scratch_shapes=[
            pltpu.VMEM((2, 4096), BF16),
            pltpu.VMEM((32, 8192), BF16),
            pltpu.SemaphoreType.DMA((17,)),
            pltpu.VMEM((256, 4608), BF16),
            pltpu.VMEM((256, 4608), BF16),
            pltpu.VMEM((256, LANES), F32),
            pltpu.VMEM((264, LANES), F32),
            pltpu.VMEM((64, 8, LANES), F32),
            pltpu.VMEM((64, 6, LANES), BF16),
        ],
        out_specs=pl.BlockSpec(memory_space=pltpu.HBM),
        compiler_params=pltpu.CompilerParams(vmem_limit_bytes=16 << 20),
        cost_estimate=pl.CostEstimate(
            flops=2 * 256 * 256 * 4608, bytes_accessed=1 << 20, transcendentals=0
        ),
        name="compress",
    )(
        pltpu.with_memory_space_constraint(echoes, pltpu.HBM),
        pltpu.with_memory_space_constraint(replica, pltpu.HBM),
    )


def migrate(quad, info, pulse):
    rows = quad[0].shape[0]
    group = lane_ids(rows) // 32
    shifted = [quad]
    for f in range(1, 4):
        rolled = [pltpu.roll(q, LANES - 32 * f, 1) for q in quad]
        shifted.append([jnp.where(group < 4 - f, rolled[k], rolled[k + 1]) for k in range(3)])
    halves = []
    for half in range(2):
        first = info[half : half + 1, :]
        width = info[2 + half : 3 + half, :]
        low = info[4 + half : 5 + half, :]
        high = info[6 + half : 7 + half, :]
        total = jnp.zeros((rows, LANES), F32)
        for step in range(8):
            inside = (first <= step) & (step < first + width)
            total = total + jnp.where(inside, shifted[step % 4][half + step // 4], 0.0)
        total = total * (1.0 / width.astype(F32))
        halves.append(jnp.where((pulse >= low) & (pulse < high), total, 0.0))
    return halves


def regroup_kernel(turned_ref, info_ref, other_ref, out_ref, quads, rows):
    quads[:, 0:6, :] = turned_ref[...].astype(F32)
    here = lax.axis_index("core")
    slot = (lax.broadcasted_iota(jnp.int32, (64, LANES), 0) + FIRST) % 64
    pulse = 8 * slot + 4 * here + lane_ids(64) // 2 % 4
    for core in range(2):
        info = jnp.where(here == core, info_ref[...], other_ref[...])
        rows[core, 0:8, :] = jnp.zeros((8, LANES), F32)
        rows[core, 136:144, :] = jnp.zeros((8, LANES), F32)
        quad = [quads[:, 2 * core + k, :] for k in range(4)]
        for half, bins in enumerate(migrate(quad, info, pulse)):
            for at, first, count in SEGMENTS:
                rows[core, pl.ds(8 + 2 * first + half, count, stride=2), :] = bins[at : at + count]
    for at, (y, core) in enumerate(LAST):
        out_ref[48 * at : 48 * at + 48, :] = rows[core, 32 * y : 32 * y + 48, :].astype(BF16)


def regroup(turned, info, other):
    return pl.pallas_call(
        regroup_kernel,
        out_shape=jax.ShapeDtypeStruct((384, LANES), BF16),
        scratch_shapes=[pltpu.VMEM((64, 8, LANES), F32), pltpu.VMEM((2, 144, LANES), F32)],
        compiler_params=pltpu.CompilerParams(vmem_limit_bytes=8 << 20),
        cost_estimate=pl.CostEstimate(flops=1 << 20, bytes_accessed=1 << 18, transcendentals=0),
        name="regroup",
    )(turned, info, other)


def bands_kernel(
    filter_ref, offset_ref, width_ref, edges_ref, out_ref, info_ref, spread, table
):
    group = lane_ids(32) // 32
    zero = jnp.zeros((32, LANES), F32)
    repeat = lane_ids(32) % 32 == lax.broadcasted_iota(jnp.int32, (32, LANES), 0)
    spread[...] = jnp.dot(
        filter_ref[...].reshape(2048, 32), repeat.astype(BF16), preferred_element_type=F32
    )

    def tap(t):
        return spread[32 * t : 32 * t + 32, :] if 0 <= t < 64 else zero

    for m in range(72):
        block = tap(m)
        for jo in range(1, 4):
            block = jnp.where(group == jo, tap(m - jo), block)
        for part in range(2):
            at = 128 * (m // 4) + 2 * (m % 4) + part
            table[pl.ds(at, 16, stride=8), :] = block[16 * part : 16 * part + 16, :]
    out_ref[...] = table[...].astype(BF16)

    def spread_bins(value):
        rows = []
        for half in range(2):
            row = jnp.full((1, LANES), value(4 * half), jnp.int32)
            for il in range(1, 4):
                row = jnp.where(group[:1] == il, value(4 * half + il), row)
            rows.append(row)
        return rows

    values = (
        lambda i: offset_ref[i],
        lambda i: width_ref[i],
        lambda i: edges_ref[0, i],
        lambda i: 512 - edges_ref[1, i],
    )
    for kind, value in enumerate(values):
        for half, row in enumerate(spread_bins(value)):
            info_ref[2 * kind + half : 2 * kind + half + 1, :] = row


def bands(filter_table, span_offset, span_width, aperture_edges):
    scalars = pl.BlockSpec(memory_space=pltpu.SMEM)
    return pl.pallas_call(
        bands_kernel,
        out_shape=(
            jax.ShapeDtypeStruct((2304, LANES), BF16),
            jax.ShapeDtypeStruct((8, LANES), jnp.int32),
        ),
        in_specs=[pl.BlockSpec(memory_space=pltpu.VMEM), scalars, scalars, scalars],
        scratch_shapes=[pltpu.VMEM((2048, LANES), F32), pltpu.VMEM((2304, LANES), F32)],
        compiler_params=pltpu.CompilerParams(vmem_limit_bytes=8 << 20),
        cost_estimate=pl.CostEstimate(flops=1 << 20, bytes_accessed=1 << 20, transcendentals=0),
        name="bands",
    )(filter_table, span_offset, span_width, aperture_edges)


def azimuth_kernel(turned_ref, bands_ref, out_ref, bins, field, pair, result, planes, final):
    bins[...] = turned_ref[...].astype(F32)
    for core in range(2):
        for half in range(2):
            arrays = [
                bins[pl.ds(48 * LAST.index((y, core)) + half, 24, stride=2), :] for y in range(4)
            ]
            for il, piece in enumerate(swap_blocks(arrays, 32)):
                field[pl.ds(8 * core + 4 * half + il, 24, stride=16), :] = piece
    field[384:392, :] = jnp.zeros((8, LANES), F32)
    pair[:, :LANES] = field[0:384, :].astype(BF16)
    pair[:, LANES:] = field[8:392, :].astype(BF16)
    steps = [pair[16 * e : 16 * e + 256, :] for e in range(9)]
    result[...] = jnp.dot(
        jnp.concatenate(steps, axis=1), bands_ref[...], preferred_element_type=F32
    )
    for half in range(2):
        arrays = [result[pl.ds(4 * half + i, 32, stride=8), :] for i in range(4)]
        for jo, piece in enumerate(swap_blocks(arrays, 32)):
            planes[pl.ds(128 * half + jo, 32, stride=4), :] = piece
        turned = planes[128 * half : 128 * half + 128, :].T
        for i in range(4):
            final[pl.ds(4 * half + i, 32, stride=8), :] = turned[32 * i : 32 * i + 32, :]
    out_ref[...] = final[...].astype(BF16)


def azimuth(turned, band_matrix):
    return pl.pallas_call(
        azimuth_kernel,
        out_shape=jax.ShapeDtypeStruct((256, LANES), BF16),
        scratch_shapes=[
            pltpu.VMEM((384, LANES), F32),
            pltpu.VMEM((392, LANES), F32),
            pltpu.VMEM((384, 256), BF16),
            pltpu.VMEM((256, LANES), F32),
            pltpu.VMEM((256, LANES), F32),
            pltpu.VMEM((256, LANES), F32),
        ],
        cost_estimate=pl.CostEstimate(
            flops=2 * 256 * 128 * 2304, bytes_accessed=1 << 20, transcendentals=0
        ),
        compiler_params=pltpu.CompilerParams(vmem_limit_bytes=8 << 20),
        name="azimuth",
    )(turned, band_matrix)


def filter_table(recon_filters):
    real = recon_filters[:, :, 0].transpose(2, 1, 0)
    imag = recon_filters[:, :, 1].transpose(2, 1, 0)
    from_real = jnp.stack([real, imag], -1).reshape(64, 16, 32)
    from_imag = jnp.stack([-imag, real], -1).reshape(64, 16, 32)
    return jnp.concatenate([from_real, from_imag], 1)


def body(echoes, replica, recon_filters, span_offset, span_width, aperture_edges):
    chunks = compress(echoes, replica)
    order = [slot + i for _, slot, count in SEGMENTS for i in range(count)]
    turned = lax.all_to_all(chunks, "slot", 0, 0, tiled=True, axis_index_groups=[order])
    _, recon_filters, span_offset, span_width, aperture_edges = lax.optimization_barrier(
        (chunks, recon_filters, span_offset, span_width, aperture_edges)
    )
    band_matrix, info = bands(
        filter_table(recon_filters), span_offset, span_width, aperture_edges
    )
    other = lax.ppermute(info, "core", [(0, 1), (1, 0)])
    windows = regroup(turned, info, other)
    gathered = lax.all_to_all(
        windows.reshape(8, 48, LANES),
        ("chan", "core"),
        0,
        0,
        tiled=True,
        axis_index_groups=[[2 * y + core for y, core in LAST]],
    )
    image = azimuth(gathered.reshape(384, LANES), band_matrix)
    return image.reshape(16, 2, 8, LANES)


def solution(mesh):
    split = Mesh(mesh.devices.reshape(64, 2, 4), ("slot", "core", "chan"))
    pulse = ("slot", "core")
    return jax.shard_map(
        body,
        mesh=split,
        in_specs=(
            P("chan", pulse, None, None),
            P(),
            P(),
            P(pulse),
            P(pulse),
            P(None, pulse),
        ),
        out_specs=P(None, None, pulse, "chan"),
        check_vma=False,
    )
```

```python
import jax
import jax.numpy as jnp
from jax import lax
from jax.experimental import pallas as pl
from jax.experimental.pallas import tpu as pltpu
from jax.sharding import Mesh
from jax.sharding import PartitionSpec as P

F32 = jnp.float32
BF16 = jnp.bfloat16
LANES = 128
NT = (((1,), (1,)), ((), ()))
FIRST = 40
LAST = ((2, 1), (3, 1), (0, 1), (1, 1), (2, 0), (3, 0), (0, 0), (1, 0))
SEGMENTS = ((0, FIRST, 64 - FIRST), (64 - FIRST, 0, FIRST))


def lane_ids(rows):
    return lax.broadcasted_iota(jnp.int32, (rows, LANES), 1)


def swap_blocks(arrays, width):
    arrays = list(arrays)
    group = lane_ids(arrays[0].shape[0]) // width
    bit = 1
    while bit < len(arrays):
        low = (group & bit) == 0
        shift = bit * width
        for first in range(len(arrays)):
            if first & bit:
                continue
            second = first | bit
            a, b = arrays[first], arrays[second]
            arrays[first] = jnp.where(low, a, pltpu.roll(b, shift, 1))
            arrays[second] = jnp.where(low, pltpu.roll(a, LANES - shift, 1), b)
        bit *= 2
    return arrays


def compress_kernel(
    echo_ref, replica_hbm, out_ref, replica_ref, echo_rows, sems, taps, windows, parts, rows, chunks, packed
):
    taps_copy = pltpu.make_async_copy(replica_hbm, replica_ref, sems.at[16])
    taps_copy.start()
    copies = [
        pltpu.make_async_copy(
            echo_ref.at[row // 4, row % 4], echo_rows.at[pl.ds(2 * row, 2), :], sems.at[row]
        )
        for row in range(16)
    ]
    for copy in copies:
        copy.start()
    taps_copy.wait()
    lane = lane_ids(32)
    shift = 4 * lax.broadcasted_iota(jnp.int32, (32, LANES), 0)
    zero = jnp.zeros((32, LANES), F32)
    for part in range(2):
        previous = zero
        for m in range(33):
            if m < 32:
                row = replica_ref[part : part + 1, m * LANES : (m + 1) * LANES].astype(F32)
                rolled = pltpu.roll(
                    jnp.broadcast_to(row, (32, LANES)), 0, 1, stride=4, stride_axis=0
                )
            else:
                rolled = zero
            tile = jnp.where(lane >= shift, rolled, previous).astype(BF16)
            previous = rolled
            for a in range(4):
                taps[
                    part * 128 + 32 * a : part * 128 + 32 * a + 32,
                    (m + a) * LANES : (m + a + 1) * LANES,
                ] = tile
        for a in range(4):
            base = part * 128 + 32 * a
            if a:
                taps[base : base + 32, : a * LANES] = jnp.zeros((32, a * LANES), BF16)
            if a < 3:
                taps[base : base + 32, (33 + a) * LANES :] = jnp.zeros(
                    (32, (3 - a) * LANES), BF16
                )
    for copy in copies:
        copy.wait()
    for w in range(8):
        windows[32 * w : 32 * w + 32, :] = echo_rows[:, 512 * w : 512 * w + 4608]
    product = lax.dot_general(taps[...], windows[...], NT, preferred_element_type=F32)
    out_copies = []
    real_lane = lane_ids(128) % 2 == 0
    for half in range(2):
        by_real = product[:128, 128 * half : 128 * half + 128]
        by_imag = product[128:, 128 * half : 128 * half + 128]
        parts[128 * half : 128 * half + 128, :] = by_real + jnp.where(
            real_lane, -pltpu.roll(by_imag, LANES - 1, 1), pltpu.roll(by_imag, 1, 1)
        )
        pieces = [parts[pl.ds(128 * half + il, 32, stride=4), :] for il in range(4)]
        for w, piece in enumerate(swap_blocks(pieces, 32)):
            at = 128 * half + 32 * w
            rows[at : at + 32, :] = piece
        if half == 0:
            rows[256:264, :] = jnp.zeros((8, LANES), F32)
        for at, slot, count in ((64 - FIRST, 0, 24),) if half == 0 else (
            (0, FIRST, 64 - FIRST),
            (88 - FIRST, 24, FIRST - 24),
        ):
            for k in range(6):
                chunks[at : at + count, k, :] = rows[pl.ds(4 * slot + k, count, stride=4), :]
            packed[at : at + count] = chunks[at : at + count, 0:6, :].astype(BF16)
            out_copies.append(
                pltpu.make_async_copy(
                    packed.at[pl.ds(at, count)], out_ref.at[pl.ds(at, count)], sems.at[at // 8]
                )
            )
            out_copies[-1].start()
    for copy in out_copies:
        copy.wait()


def compress(echoes, replica):
    return pl.pallas_call(
        compress_kernel,
        out_shape=jax.ShapeDtypeStruct((64, 6, LANES), BF16),
        in_specs=[
            pl.BlockSpec(memory_space=pltpu.HBM),
            pl.BlockSpec(memory_space=pltpu.HBM),
        ],
        scratch_shapes=[
            pltpu.VMEM((2, 4096), BF16),
            pltpu.VMEM((32, 8192), BF16),
            pltpu.SemaphoreType.DMA((17,)),
            pltpu.VMEM((256, 4608), BF16),
            pltpu.VMEM((256, 4608), BF16),
            pltpu.VMEM((256, LANES), F32),
            pltpu.VMEM((264, LANES), F32),
            pltpu.VMEM((64, 8, LANES), F32),
            pltpu.VMEM((64, 6, LANES), BF16),
        ],
        out_specs=pl.BlockSpec(memory_space=pltpu.HBM),
        compiler_params=pltpu.CompilerParams(vmem_limit_bytes=16 << 20),
        cost_estimate=pl.CostEstimate(
            flops=2 * 256 * 256 * 4608, bytes_accessed=1 << 20, transcendentals=0
        ),
        name="compress",
    )(
        pltpu.with_memory_space_constraint(echoes, pltpu.HBM),
        pltpu.with_memory_space_constraint(replica, pltpu.HBM),
    )


def migrate(quad, info, pulse):
    rows = quad[0].shape[0]
    group = lane_ids(rows) // 32
    shifted = [quad]
    for f in range(1, 4):
        rolled = [pltpu.roll(q, LANES - 32 * f, 1) for q in quad]
        shifted.append([jnp.where(group < 4 - f, rolled[k], rolled[k + 1]) for k in range(3)])
    halves = []
    for half in range(2):
        first = info[half : half + 1, :]
        width = info[2 + half : 3 + half, :]
        low = info[4 + half : 5 + half, :]
        high = info[6 + half : 7 + half, :]
        total = jnp.zeros((rows, LANES), F32)
        for step in range(8):
            inside = (first <= step) & (step < first + width)
            total = total + jnp.where(inside, shifted[step % 4][half + step // 4], 0.0)
        total = total * (1.0 / width.astype(F32))
        halves.append(jnp.where((pulse >= low) & (pulse < high), total, 0.0))
    return halves


def regroup_kernel(turned_ref, info_ref, other_ref, out_ref, quads, rows):
    quads[:, 0:6, :] = turned_ref[...].astype(F32)
    here = lax.axis_index("core")
    slot = (lax.broadcasted_iota(jnp.int32, (64, LANES), 0) + FIRST) % 64
    pulse = 8 * slot + 4 * here + lane_ids(64) // 2 % 4
    for core in range(2):
        info = jnp.where(here == core, info_ref[...], other_ref[...])
        rows[core, 0:8, :] = jnp.zeros((8, LANES), F32)
        rows[core, 136:144, :] = jnp.zeros((8, LANES), F32)
        quad = [quads[:, 2 * core + k, :] for k in range(4)]
        for half, bins in enumerate(migrate(quad, info, pulse)):
            for at, first, count in SEGMENTS:
                rows[core, pl.ds(8 + 2 * first + half, count, stride=2), :] = bins[at : at + count]
    for at, (y, core) in enumerate(LAST):
        out_ref[48 * at : 48 * at + 48, :] = rows[core, 32 * y : 32 * y + 48, :].astype(BF16)


def regroup(turned, info, other):
    return pl.pallas_call(
        regroup_kernel,
        out_shape=jax.ShapeDtypeStruct((384, LANES), BF16),
        scratch_shapes=[pltpu.VMEM((64, 8, LANES), F32), pltpu.VMEM((2, 144, LANES), F32)],
        compiler_params=pltpu.CompilerParams(vmem_limit_bytes=8 << 20),
        cost_estimate=pl.CostEstimate(flops=1 << 20, bytes_accessed=1 << 18, transcendentals=0),
        name="regroup",
    )(turned, info, other)


def bands_kernel(
    filter_ref, offset_ref, width_ref, edges_ref, out_ref, info_ref, spread, table
):
    group = lane_ids(32) // 32
    zero = jnp.zeros((32, LANES), F32)
    repeat = lane_ids(32) % 32 == lax.broadcasted_iota(jnp.int32, (32, LANES), 0)
    spread[...] = jnp.dot(
        filter_ref[...].reshape(2048, 32), repeat.astype(BF16), preferred_element_type=F32
    )

    def tap(t):
        return spread[32 * t : 32 * t + 32, :] if 0 <= t < 64 else zero

    for m in range(72):
        block = tap(m)
        for jo in range(1, 4):
            block = jnp.where(group == jo, tap(m - jo), block)
        for part in range(2):
            at = 128 * (m // 4) + 2 * (m % 4) + part
            table[pl.ds(at, 16, stride=8), :] = block[16 * part : 16 * part + 16, :]
    out_ref[...] = table[...].astype(BF16)

    def spread_bins(value):
        rows = []
        for half in range(2):
            row = jnp.full((1, LANES), value(4 * half), jnp.int32)
            for il in range(1, 4):
                row = jnp.where(group[:1] == il, value(4 * half + il), row)
            rows.append(row)
        return rows

    values = (
        lambda i: offset_ref[i],
        lambda i: width_ref[i],
        lambda i: edges_ref[0, i],
        lambda i: 512 - edges_ref[1, i],
    )
    for kind, value in enumerate(values):
        for half, row in enumerate(spread_bins(value)):
            info_ref[2 * kind + half : 2 * kind + half + 1, :] = row


def bands(filter_table, span_offset, span_width, aperture_edges):
    scalars = pl.BlockSpec(memory_space=pltpu.SMEM)
    return pl.pallas_call(
        bands_kernel,
        out_shape=(
            jax.ShapeDtypeStruct((2304, LANES), BF16),
            jax.ShapeDtypeStruct((8, LANES), jnp.int32),
        ),
        in_specs=[pl.BlockSpec(memory_space=pltpu.VMEM), scalars, scalars, scalars],
        scratch_shapes=[pltpu.VMEM((2048, LANES), F32), pltpu.VMEM((2304, LANES), F32)],
        compiler_params=pltpu.CompilerParams(vmem_limit_bytes=8 << 20),
        cost_estimate=pl.CostEstimate(flops=1 << 20, bytes_accessed=1 << 20, transcendentals=0),
        name="bands",
    )(filter_table, span_offset, span_width, aperture_edges)


def azimuth_kernel(turned_ref, bands_ref, out_ref, bins, field, pair, result, planes, final):
    bins[...] = turned_ref[...].astype(F32)
    for core in range(2):
        for half in range(2):
            arrays = [
                bins[pl.ds(48 * LAST.index((y, core)) + half, 24, stride=2), :] for y in range(4)
            ]
            for il, piece in enumerate(swap_blocks(arrays, 32)):
                field[pl.ds(8 * core + 4 * half + il, 24, stride=16), :] = piece
    field[384:392, :] = jnp.zeros((8, LANES), F32)
    pair[:, :LANES] = field[0:384, :].astype(BF16)
    pair[:, LANES:] = field[8:392, :].astype(BF16)
    steps = [pair[16 * e : 16 * e + 256, :] for e in range(8)] + [pair[128:384, :LANES]]
    result[...] = jnp.dot(
        jnp.concatenate(steps, axis=1), bands_ref[0:2176, :], preferred_element_type=F32
    )
    for half in range(2):
        arrays = [result[pl.ds(4 * half + i, 32, stride=8), :] for i in range(4)]
        for jo, piece in enumerate(swap_blocks(arrays, 32)):
            planes[pl.ds(128 * half + jo, 32, stride=4), :] = piece
        turned = planes[128 * half : 128 * half + 128, :].T
        for i in range(4):
            final[pl.ds(4 * half + i, 32, stride=8), :] = turned[32 * i : 32 * i + 32, :]
    out_ref[...] = final[...].astype(BF16)


def azimuth(turned, band_matrix):
    return pl.pallas_call(
        azimuth_kernel,
        out_shape=jax.ShapeDtypeStruct((256, LANES), BF16),
        scratch_shapes=[
            pltpu.VMEM((384, LANES), F32),
            pltpu.VMEM((392, LANES), F32),
            pltpu.VMEM((384, 256), BF16),
            pltpu.VMEM((256, LANES), F32),
            pltpu.VMEM((256, LANES), F32),
            pltpu.VMEM((256, LANES), F32),
        ],
        cost_estimate=pl.CostEstimate(
            flops=2 * 256 * 128 * 2304, bytes_accessed=1 << 20, transcendentals=0
        ),
        compiler_params=pltpu.CompilerParams(vmem_limit_bytes=8 << 20),
        name="azimuth",
    )(turned, band_matrix)


def filter_table(recon_filters):
    real = recon_filters[:, :, 0].transpose(2, 1, 0)
    imag = recon_filters[:, :, 1].transpose(2, 1, 0)
    from_real = jnp.stack([real, imag], -1).reshape(64, 16, 32)
    from_imag = jnp.stack([-imag, real], -1).reshape(64, 16, 32)
    return jnp.concatenate([from_real, from_imag], 1)


def body(echoes, replica, recon_filters, span_offset, span_width, aperture_edges):
    chunks = compress(echoes, replica)
    order = [slot + i for _, slot, count in SEGMENTS for i in range(count)]
    turned = lax.all_to_all(chunks, "slot", 0, 0, tiled=True, axis_index_groups=[order])
    _, recon_filters, span_offset, span_width, aperture_edges = lax.optimization_barrier(
        (chunks, recon_filters, span_offset, span_width, aperture_edges)
    )
    band_matrix, info = bands(
        filter_table(recon_filters), span_offset, span_width, aperture_edges
    )
    other = lax.ppermute(info, "core", [(0, 1), (1, 0)])
    windows = regroup(turned, info, other)
    gathered = lax.all_to_all(
        windows.reshape(8, 48, LANES),
        ("chan", "core"),
        0,
        0,
        tiled=True,
        axis_index_groups=[[2 * y + core for y, core in LAST]],
    )
    image = azimuth(gathered.reshape(384, LANES), band_matrix)
    return image.reshape(16, 2, 8, LANES)


def solution(mesh):
    split = Mesh(mesh.devices.reshape(64, 2, 4), ("slot", "core", "chan"))
    pulse = ("slot", "core")
    return jax.shard_map(
        body,
        mesh=split,
        in_specs=(
            P("chan", pulse, None, None),
            P(),
            P(),
            P(pulse),
            P(pulse),
            P(None, pulse),
        ),
        out_specs=P(None, None, pulse, "chan"),
        check_vma=False,
    )
```
